128 devices in a mesh: seq: 8 (over x, core), tensor: 16 (over y, z).
Axes of the slice: x: 4, y: 4, z: 4, core: 2. Of those that a mesh axis runs over, the one named last changes fastest.
Arguments:
- hidden_in: bfloat16 [8192, 2048], P('seq'), may hold values from -6 to 6
- gain_attn: float32 [2048], replicated, may hold values from 0.1 to 1.9
- gain_mlp: float32 [2048], replicated, may hold values from 0.1 to 1.9
- w_qkv: bfloat16 [3, 2048, 2048], P(None, None, 'tensor')
- w_attn_out: bfloat16 [2048, 2048], P('tensor'), may hold values from -0.125 to 0.125
- w_mlp_in: bfloat16 [2048, 8192], P(None, 'tensor'), may hold values from -0.125 to 0.125
- w_mlp_out: bfloat16 [8192, 2048], P('tensor'), may hold values from -0.0625 to 0.0625
- segment_ids: int32 [8192], P('seq'), may hold values from 0 to 1, as said below
- positions: int32 [8192], P('seq'), may hold values from 0 to 8191, as said below
- kv_prefill: bfloat16 [128, 8, 2, 64, 2048], P('seq', None, None, None, 'tensor'), may hold values from -6 to 6
- page_source: int32 [128], replicated, may hold values from 0 to 127, as said below
Outputs:
- hidden_out: bfloat16 [8192, 2048], P('seq')
- kv_decode: bfloat16 [128, 8, 2, 64, 2048], P('tensor', None, None, None, 'seq')
The draws below stay inside these ranges and needn't reach their ends.
Inputs may be any that keep to these rules, and one draw needn't show every extreme that they name: `segment_ids`: never falling along the span; two prompts, each a multiple of 64 tokens long, the first of 2048 to 6144 tokens. `positions`: within a prompt, consecutive from the prompt's first position; the second prompt starts at 0 and the first at the second prompt's length. `page_source`: a permutation; page g * 8 + r + j (j below 1, r below 8) takes a block of the r-th aligned run of 16 blocks.
All inputs are finite; a program needn't handle non-finite values.
Results may differ from the reference program's by a relative error of at most 0.015.
The reference program's roundings to bfloat16 on the way (of `normed_attn`, `normed_mlp`, `weights`, `attended` and `hidden_mlp`) count: a program that leaves them out, or rounds other values in their place, can miss the bound.
Values may be sent and summed in bfloat16 or wider, within the bound.
A program may use at most 128 MiB of HBM per device.

```python
import jax
import jax.numpy as jnp
from jax import lax

D = 2048
HEADS = 8
HD = 256
FF = 8192
TOK_DEV = 1024
SHORT = 64
LAYERS = 8
BLK = 64
PG_DEV = 1
TOKENS = 8192
LONG = 4096
PAGES_ROW = 16
CBLOCKS = 128


def span_layout(key):
    base_key = jax.random.fold_in(key, 11)
    unit_count = LONG // SHORT
    first_length = (jax.random.randint(base_key, (), unit_count // 2, unit_count + unit_count // 2 + 1) * SHORT).astype(jnp.int32)
    token_ids = jnp.arange(TOKENS, dtype=jnp.int32)
    seg_ids = (token_ids >= first_length).astype(jnp.int32)
    position_ids = jnp.where(seg_ids == 0, token_ids + (TOKENS - first_length), token_ids - first_length).astype(jnp.int32)
    return (seg_ids, position_ids)


def draw_segment_ids(key, part):
    return span_layout(key)[0]


def draw_positions(key, part):
    return span_layout(key)[1]


def draw_page_source(key, part):
    row_count = CBLOCKS // PAGES_ROW
    group_count = PAGES_ROW // PG_DEV
    row_keys = jax.random.split(jax.random.fold_in(key, 5), row_count)
    orders = jax.vmap(lambda row_key: jax.random.permutation(row_key, PAGES_ROW))(row_keys).astype(jnp.int32)
    offsets = jnp.arange(row_count, dtype=jnp.int32)[:, None] * PAGES_ROW
    blocks = (orders + offsets).reshape(row_count, group_count, PG_DEV)
    return jnp.transpose(blocks, (1, 0, 2)).reshape(CBLOCKS).astype(jnp.int32)


def draw_w_qkv(key, part):
    base = jax.random.normal(key, (3, D, HEADS * HD), jnp.float32) * D ** (-0.5)
    return base.astype(jnp.bfloat16)


def steps_of(own_key, shape, pieces, low, top_value):
    loudness = 1.0
    for dim, blocks in pieces:
        steps = jax.random.uniform(jax.random.fold_in(jax.random.fold_in(own_key, 6), dim), (blocks,), jnp.float32, low / len(pieces), top_value / len(pieces))
        loudness = loudness * jnp.repeat(jnp.exp(steps), shape[dim] // blocks).reshape((-1,) + (1,) * (len(shape) - 1 - dim))
    return loudness


def noise(key, dims, deviation, bound, cuts=(), held_as=jnp.bfloat16):
    values = deviation * jax.random.normal(key, dims, jnp.float32)
    if cuts:
        values = values * steps_of(key, dims, cuts, -0.22, 0.18)
    return jnp.clip(values, -bound, bound).astype(held_as)


def setup_inputs(seed: int = 0) -> dict:
    seeds = jax.random.split(jax.random.key(seed), 12)
    return {
        "hidden_in": noise(seeds[0], (TOKENS, D), 1.0, 6.0, ((0, 8),)),
        "gain_attn": jnp.clip(1.0 + 0.18 * jax.random.normal(seeds[1], (D,), jnp.float32), 0.1, 1.9),
        "gain_mlp": jnp.clip(1.0 + 0.18 * jax.random.normal(seeds[2], (D,), jnp.float32), 0.1, 1.9),
        "w_qkv": draw_w_qkv(jax.random.fold_in(seeds[11], 71), 0),
        "w_attn_out": noise(seeds[4], (HEADS * HD, D), (HEADS * HD) ** -0.5, 0.125, ((0, 16),)),
        "w_mlp_in": noise(seeds[5], (D, FF), D ** -0.5, 0.125, ((1, 16),)),
        "w_mlp_out": noise(seeds[6], (FF, D), FF ** -0.5, 0.0625, ((0, 16),)),
        "segment_ids": draw_segment_ids(jax.random.fold_in(seeds[11], 71), 0),
        "positions": draw_positions(jax.random.fold_in(seeds[11], 71), 0),
        "kv_prefill": noise(seeds[9], (CBLOCKS, LAYERS, 2, BLK, D), 1.0, 6.0, ((0, 8), (4, 16))),
        "page_source": draw_page_source(jax.random.fold_in(seeds[11], 71), 0),
    }


def layer_norm(values, gain_vec):
    mean_val = lax.optimization_barrier(jnp.mean(values, axis=-1, keepdims=True))
    centered = values - mean_val
    spread_sq = lax.optimization_barrier(jnp.mean(centered * centered, axis=-1, keepdims=True))
    return centered * lax.rsqrt(spread_sq + 1e-05) * gain_vec

def rotate(values, positions):
    rot_dims = HD // 4
    half_dims = rot_dims // 2
    freqs = 10000.0 ** (-(jnp.arange(half_dims, dtype=jnp.float32) * 2.0 / rot_dims))
    angles = positions.astype(jnp.float32)[:, None] * freqs[None, :]
    cosine = jnp.cos(angles)
    sine = jnp.sin(angles)
    first_half = values[:, :half_dims]
    second_half = values[:, half_dims:rot_dims]
    return jnp.concatenate([first_half * cosine - second_half * sine, second_half * cosine + first_half * sine, values[:, rot_dims:]], axis=1)

def reference(hidden_in, gain_attn, gain_mlp, w_qkv, w_attn_out, w_mlp_in, w_mlp_out, segment_ids, positions, kv_prefill, page_source):
    kv_decode = jnp.take(kv_prefill, page_source.astype(jnp.int32), axis=0)
    values = hidden_in.astype(jnp.float32)
    normed_attn = layer_norm(values, gain_attn).astype(jnp.bfloat16)
    normed_mlp = layer_norm(values, gain_mlp).astype(jnp.bfloat16)
    proj_query = jnp.dot(normed_attn, w_qkv[0], preferred_element_type=jnp.float32).reshape(TOKENS, HEADS, HD)
    proj_key = jnp.dot(normed_attn, w_qkv[1], preferred_element_type=jnp.float32).reshape(TOKENS, HEADS, HD)
    proj_val = jnp.dot(normed_attn, w_qkv[2], preferred_element_type=jnp.float32).reshape(TOKENS, HEADS, HD)
    rotate_heads = jax.vmap(rotate, in_axes=(1, None), out_axes=1)
    queries = rotate_heads(proj_query, positions).astype(jnp.bfloat16)
    keys_all = rotate_heads(proj_key, positions).astype(jnp.bfloat16)
    vals_all = proj_val.astype(jnp.bfloat16)
    token_ids = jnp.arange(TOKENS, dtype=jnp.int32)
    scale = HD ** (-0.5)

    def head_attention(operands):
        q_head, k_head, v_head = operands

        def query_block(block_index):
            first_row = (block_index * TOK_DEV).astype(jnp.int32)
            q_block = lax.dynamic_slice_in_dim(q_head, first_row, TOK_DEV, 0)
            row_ids = first_row + jnp.arange(TOK_DEV, dtype=jnp.int32)
            row_segs = lax.dynamic_slice_in_dim(segment_ids, first_row, TOK_DEV, 0)
            scores = jnp.dot(q_block, k_head.T, preferred_element_type=jnp.float32) * scale
            allowed = (segment_ids[None, :] == row_segs[:, None]) & (token_ids[None, :] <= row_ids[:, None])
            scores = jnp.where(allowed, scores, -1e+30)
            peak = lax.optimization_barrier(jnp.max(scores, axis=1, keepdims=True))
            weights = jnp.where(allowed, jnp.exp(scores - peak), 0.0)
            denom = lax.optimization_barrier(jnp.sum(weights, axis=1, keepdims=True))
            summed = jnp.dot(weights.astype(jnp.bfloat16), v_head, preferred_element_type=jnp.float32)
            return (summed / denom).astype(jnp.bfloat16)
        blocks_out = lax.map(query_block, jnp.arange(TOKENS // TOK_DEV, dtype=jnp.int32))
        return blocks_out.reshape(TOKENS, HD)
    attended = lax.map(head_attention, (jnp.transpose(queries, (1, 0, 2)), jnp.transpose(keys_all, (1, 0, 2)), jnp.transpose(vals_all, (1, 0, 2))))
    attended = jnp.transpose(attended, (1, 0, 2)).reshape(TOKENS, HEADS * HD)
    attn_sum = jnp.dot(attended, w_attn_out, preferred_element_type=jnp.float32)
    hidden_mlp = jax.nn.gelu(jnp.dot(normed_mlp, w_mlp_in, preferred_element_type=jnp.float32), approximate=False).astype(jnp.bfloat16)
    mlp_sum = jnp.dot(hidden_mlp, w_mlp_out, preferred_element_type=jnp.float32)
    hidden_out = (values + attn_sum + mlp_sum).astype(jnp.bfloat16)
    return (hidden_out, kv_decode)
```

```python
import jax
import jax.numpy as jnp
from jax import lax
from jax.experimental import pallas as pl
from jax.experimental.pallas import tpu as pltpu
from jax.sharding import PartitionSpec as P

MESH = pl.DeviceIdType.MESH
F32 = jnp.float32
BF16 = jnp.bfloat16
HD = 256
LOW = -1e30
MASKED = -3e30
TT = (((1,), (1,)), ((), ()))
FF = (((0,), (0,)), ((), ()))


def layer_kernel(
    x_hbm,
    ga_ref,
    gm_ref,
    wqkv_hbm,
    wo_hbm,
    wi_hbm,
    w2_hbm,
    cos_ref,
    sin_ref,
    first_ref,
    psrc_ref,
    kv_hbm,
    out_hbm,
    kvout_hbm,
    x_v,
    na_v,
    nm_v,
    wcat_v,
    wi_v,
    w2_v,
    wo_v,
    hid_v,
    part_v,
    kvin_v,
    kvs_v,
    bufa_v,
    bufb_v,
    kvx_v,
    kvbuf_v,
    stage_v,
    qstage_v,
    q_v,
    acc_v,
    stat_v,
    mine_v,
    theirs_v,
    direct_v,
    relay_v,
    sums_v,
    merged_v,
    fold_v,
    direct2_v,
    relay2_v,
    sums2_v,
    merged2_v,
    lsem,
    ssem,
    rsem,
    kvs_sem,
    kvr_sem,
):
    seq = lax.axis_index("seq")
    ten = lax.axis_index("tensor")
    xx = seq // 2
    core = lax.rem(seq, 2)
    yy = ten // 4
    zz = lax.rem(ten, 4)
    half = lax.rem(ten, 2)
    zh = zz // 2

    def around(value, step):
        return lax.rem(value + step + 4, 4)

    def dev(x_=None, c_=None, y_=None, z_=None):
        x_ = xx if x_ is None else x_
        c_ = core if c_ is None else c_
        y_ = yy if y_ is None else y_
        z_ = zz if z_ is None else z_
        return (x_ * 2 + c_, y_ * 4 + z_)

    counter = [0]
    pending = []

    def remote(src, dst, device):
        index = counter[0]
        counter[0] += 1
        copy = pltpu.make_async_remote_copy(
            src_ref=src,
            dst_ref=dst,
            send_sem=ssem.at[index],
            recv_sem=rsem.at[index],
            device_id=device,
            device_id_type=MESH,
        )
        pending.append(copy)
        return copy

    local_count = [0]

    def local(src, dst):
        index = local_count[0]
        local_count[0] += 1
        copy = pltpu.make_async_copy(src, dst, lsem.at[index])
        copy.start()
        return copy

    load_x = local(x_hbm, x_v)
    load_w = [local(wqkv_hbm.at[c], wcat_v.at[:, pl.ds(j * 128, 128)]) for j, c in ((0, 1), (1, 2), (2, 0))]
    load_kv = local(kv_hbm, kvin_v)
    load_wi = local(wi_hbm, wi_v)
    load_w2 = local(w2_hbm, w2_v)
    own_rows = pl.ds(pl.multiple_of(half * 128, 128), 128)
    load_wo = local(wo_hbm, wo_v.at[own_rows, :])

    barrier = pltpu.get_barrier_semaphore()
    peers = [dev(y_=around(yy, k)) for k in (1, 2, 3)]
    peers += [dev(z_=around(zz, k)) for k in (1, 2, 3)]
    peers += [(lax.rem(seq + k, 8), ten) for k in range(1, 8)]
    for peer in peers:
        pl.semaphore_signal(barrier, inc=1, device_id=peer, device_id_type=MESH)
    pl.semaphore_wait(barrier, len(peers))

    partner = dev(z_=zz + 1 - 2 * half)
    twin = (seq + 1 - 2 * core, ten)

    half_rows = pl.ds(pl.multiple_of(half * 128 + core * 64, 64), 64)
    wo_cross = remote(wo_hbm.at[pl.ds(pl.multiple_of(core * 64, 64), 64)], wo_v.at[half_rows, :], partner)
    wo_cross.start()

    load_kv.wait()

    @pl.loop(0, 16)
    def _(group):
        kvs_v[group] = kvin_v[lax.rem(psrc_ref[group * 8 + seq], 16)]

    low = pl.ds(0, 512)
    high = pl.ds(512, 512)
    col_half = pl.ds(pl.multiple_of(half * 128, 128), 128)
    a_one = []
    for k in (1, 2, 3):
        to_y = around(yy, k)
        a_one.append(remote(kvs_v.at[pl.ds(to_y * 4, 4), low], bufa_v.at[yy], dev(y_=to_y)))
        a_one[-1].start()
    a_own = local(kvs_v.at[pl.ds(yy * 4, 4), low], bufa_v.at[yy])

    load_x.wait()
    for copy in load_w:
        copy.wait()
    ga = ga_ref[...]
    gm = gm_ref[...]

    @pl.loop(0, 4)
    def _(step):
        start = lax.rem(step * 256 + (1 - half) * 512, 1024)
        rows = pl.ds(pl.multiple_of(start, 256), 256)
        values = x_v[rows, :].astype(F32)
        mean = jnp.mean(values, axis=-1, keepdims=True)
        centered = values - mean
        spread = jnp.mean(centered * centered, axis=-1, keepdims=True)
        normed = centered * lax.rsqrt(spread + 1e-05)
        na = (normed * ga).astype(BF16)
        na_v[rows, :] = na
        nm_v[rows, :] = (normed * gm).astype(BF16)
        kv = jnp.dot(na, wcat_v[:, 0:256], preferred_element_type=F32)
        q = jnp.dot(na, wcat_v[:, 256:384], preferred_element_type=F32)
        lanes = lax.broadcasted_iota(jnp.int32, (256, 128), 1)
        cosine = cos_ref[rows, :]
        sine = sin_ref[rows, :]

        def turned(values_in):
            other = jnp.where(lanes < 32, pltpu.roll(values_in, 96, 1), pltpu.roll(values_in, 32, 1))
            return values_in * cosine + other * sine

        stage_v[0, rows, :] = turned(kv[:, 0:128]).astype(BF16)
        stage_v[1, rows, :] = kv[:, 128:256].astype(BF16)
        qstage_v[rows, :] = (turned(q) * (HD**-0.5)).astype(BF16)

    own_keys = pl.ds(pl.multiple_of(half * 512, 512), 512)
    cross_keys = pl.ds(pl.multiple_of((1 - half) * 512, 512), 512)
    kv_cross = remote(stage_v.at[:, cross_keys], kvbuf_v.at[seq, :, :, col_half], partner)
    kv_cross.start()
    q_cross = remote(qstage_v, q_v.at[:, col_half], partner)
    q_cross.start()
    kv_own = local(stage_v.at[:, own_keys], kvbuf_v.at[seq, :, :, col_half])
    q_own = local(qstage_v, q_v.at[:, col_half])

    b_one = []
    for k in (1, 2, 3):
        to_z = around(zz, k)
        b_one.append(
            [
                remote(kvs_v.at[y4 * 4 + to_z, high], bufb_v.at[y4, zh, :, col_half], dev(z_=to_z))
                for y4 in range(4)
            ]
        )
    for copies in b_one:
        for copy in copies:
            copy.start()
    b_own = [local(kvs_v.at[y4 * 4 + zz, high], bufb_v.at[y4, zh, :, col_half]) for y4 in range(4)]

    load_wi.wait()

    @pl.loop(0, 4)
    def _(step):
        rows = pl.ds(pl.multiple_of(step * 256, 256), 256)
        hidden = jnp.dot(nm_v[rows, :], wi_v[...], preferred_element_type=F32)
        hid_v[rows, :] = (0.5 * hidden * (1.0 + lax.erf(hidden * (0.5**0.5)))).astype(BF16)

    kv_own.wait()
    kv_cross.wait_recv()

    def kv_send(slot, device):
        return pltpu.make_async_remote_copy(
            src_ref=kvbuf_v.at[slot],
            dst_ref=kvbuf_v.at[slot],
            send_sem=kvs_sem.at[slot],
            recv_sem=kvr_sem.at[slot],
            device_id=device,
            device_id_type=MESH,
        )

    def kv_out(slot, device, index):
        return pltpu.make_async_remote_copy(
            src_ref=kvbuf_v.at[slot],
            dst_ref=kvbuf_v.at[slot],
            send_sem=kvs_sem.at[8 + index],
            recv_sem=kvr_sem.at[slot],
            device_id=device,
            device_id_type=MESH,
        )

    for k in (1, 2, 3):
        pl.when(xx + k < 4)(kv_out(seq, dev(x_=lax.rem(xx + k, 4)), k).start)
    pl.when(core == 0)(kv_out(seq, twin, 0).start)

    load_w2.wait()

    @pl.loop(0, 4)
    def _(step):
        rows = pl.ds(pl.multiple_of(step * 256, 256), 256)
        part_v[rows, :] = jnp.dot(hid_v[rows, :], w2_v[...], preferred_element_type=F32).astype(BF16)

    acc_v[...] = jnp.zeros_like(acc_v)
    stat_v[0:1, :] = jnp.full((1, 1024), LOW, F32)
    stat_v[1:2, :] = jnp.zeros((1, 1024), F32)

    def attend(slot):
        keys = kvbuf_v[slot, 0]
        vals = kvbuf_v[slot, 1]
        vals_t = vals.T
        key_ids = slot * 1024 + half * 512 + lax.broadcasted_iota(jnp.int32, (512, 1), 0)

        @pl.loop(0, 4)
        def _(step):
            cols = pl.ds(pl.multiple_of(step * 256, 256), 256)
            scores = lax.dot_general(keys, q_v[cols, :], TT, preferred_element_type=F32)
            query_ids = seq * 1024 + step * 256 + lax.broadcasted_iota(jnp.int32, (1, 256), 1)
            allowed = (key_ids >= first_ref[:, cols]) & (key_ids <= query_ids)
            scores = jnp.where(allowed, scores, MASKED)
            old_max = stat_v[0:1, cols]
            new_max = jnp.maximum(old_max, jnp.max(scores, axis=0, keepdims=True))
            weights = jnp.exp(scores - new_max)
            keep = jnp.exp(old_max - new_max)
            stat_v[0:1, cols] = new_max
            stat_v[1:2, cols] = stat_v[1:2, cols] * keep + jnp.sum(weights, axis=0, keepdims=True)
            acc_v[:, cols] = acc_v[:, cols] * keep + jnp.dot(
                vals_t, weights.astype(BF16), preferred_element_type=F32
            )

    q_own.wait()
    q_cross.wait_recv()
    attend(seq)

    a_own.wait()
    for copy in a_one:
        copy.wait_recv()
    a_two = []
    for k in (1, 2, 3):
        to_z = around(zz, k)
        a_two.append(remote(bufa_v.at[:, to_z], kvx_v.at[:, zh, low, col_half], dev(z_=to_z)))
        a_two[-1].start()
    a_two_own = local(bufa_v.at[:, zz], kvx_v.at[:, zh, low, col_half])
    for copy in b_own:
        copy.wait()
    for copies in b_one:
        for copy in copies:
            copy.wait_recv()
    b_two = []
    for k in (1, 2, 3):
        to_y = around(yy, k)
        b_two.append(remote(bufb_v.at[to_y], kvx_v.at[yy, :, high, :], dev(y_=to_y)))
        b_two[-1].start()
    b_two_own = local(bufb_v.at[yy], kvx_v.at[yy, :, high, :])

    @pl.when(core == 1)
    def _():
        kv_send(seq - 1, twin).wait_recv()
        attend(seq - 1)

    @pl.loop(0, xx)
    def _(step):
        base = 2 * (xx - 1 - step)
        kv_send(base + core, twin).wait_recv()
        kv_send(base + core, twin).start()
        attend(base + core)
        kv_send(base + 1 - core, twin).wait_recv()
        attend(base + 1 - core)

    mine_v[...] = stat_v[...]
    stat_cross = remote(mine_v, theirs_v, partner)
    stat_cross.start()
    load_wo.wait()
    wo_cross.wait_recv()
    wo_twin = remote(wo_v.at[pl.ds(pl.multiple_of((1 - half) * 128 + core * 64, 64), 64), :],
                     wo_v.at[pl.ds(pl.multiple_of((1 - half) * 128 + core * 64, 64), 64), :], twin)
    wo_twin.start()
    wo_twin.wait_recv()
    stat_cross.wait_recv()
    top = jnp.maximum(stat_v[0:1, :], theirs_v[0:1, :])
    mine = jnp.exp(stat_v[0:1, :] - top)
    total = stat_v[1:2, :] * mine + theirs_v[1:2, :] * jnp.exp(theirs_v[0:1, :] - top)
    stat_v[0:1, :] = mine / total

    @pl.loop(0, 4)
    def _(step):
        cols = pl.ds(pl.multiple_of(step * 256, 256), 256)
        attended = (acc_v[:, cols] * stat_v[0:1, cols]).astype(BF16)
        summed = lax.dot_general(attended, wo_v[...], FF, preferred_element_type=F32)
        part_v[cols, :] = (part_v[cols, :].astype(F32) + summed).astype(BF16)

    def cols_of(which):
        return pl.ds(which * 1024, 1024)

    def axis_dev(which, step, first):
        along_y = (which == 0) == first
        return dev(y_=around(yy, step)) if along_y else dev(z_=around(zz, step))

    def scatter(which, first, source, size, direct, relay, sums, merged):
        pos = yy if (which == 0) == first else zz
        hs = size // 2

        def piece(step, part):
            begin = around(pos, step) * size + part * hs
            return source(pl.ds(pl.multiple_of(begin, hs), hs))

        plus = axis_dev(which, 1, first)
        minus = axis_dev(which, -1, first)
        r0 = remote(piece(2, 0), relay.at[which, 0], plus)
        r1 = remote(piece(2, 1), relay.at[which, 1], minus)
        d0 = remote(piece(1, 1), direct.at[which, 0], plus)
        d1 = remote(piece(-1, 0), direct.at[which, 1], minus)
        m0 = remote(sums.at[which, 0], merged.at[which, 0], plus)
        m1 = remote(sums.at[which, 1], merged.at[which, 1], minus)

        def one():
            for copy in (r0, r1, d0, d1):
                copy.start()

        def two():
            r0.wait_recv()
            sums[which, 0] = (piece(1, 0)[...].astype(F32) + relay[which, 0].astype(F32)).astype(BF16)
            m0.start()
            r1.wait_recv()
            sums[which, 1] = (piece(-1, 1)[...].astype(F32) + relay[which, 1].astype(F32)).astype(BF16)
            m1.start()

        def three():
            d0.wait_recv()
            d1.wait_recv()
            m0.wait_recv()
            m1.wait_recv()
            lower = piece(0, 0)[...].astype(F32) + direct[which, 1].astype(F32) + merged[which, 0].astype(F32)
            upper = piece(0, 1)[...].astype(F32) + direct[which, 0].astype(F32) + merged[which, 1].astype(F32)
            return lower, upper

        return one, two, three

    first_stage = [
        scatter(w, True, lambda rows, w=w: part_v.at[rows, cols_of(w)], 256, direct_v, relay_v, sums_v, merged_v)
        for w in (0, 1)
    ]
    second_stage = [
        scatter(w, False, lambda rows, w=w: fold_v.at[w, rows], 64, direct2_v, relay2_v, sums2_v, merged2_v)
        for w in (0, 1)
    ]
    for stage in first_stage:
        stage[0]()
    for stage in first_stage:
        stage[1]()
    for w in (0, 1):
        lower, upper = first_stage[w][2]()
        fold_v[w, 0:128] = lower.astype(BF16)
        fold_v[w, 128:256] = upper.astype(BF16)
        second_stage[w][0]()
    for stage in second_stage:
        stage[1]()

    base_of = (yy * 256, zz * 256)
    small_of = (zz, yy)

    def gather(which, first, base, size):
        pos = yy if (which == 0) == first else zz
        hs = size // 2

        def rows_at(step, part=None):
            begin = base + around(pos, step) * size
            if part is None:
                return na_v.at[pl.ds(pl.multiple_of(begin, size), size), cols_of(which)]
            return na_v.at[pl.ds(pl.multiple_of(begin + part * hs, hs), hs), cols_of(which)]

        plus = axis_dev(which, 1, first)
        minus = axis_dev(which, -1, first)
        own = rows_at(0)
        g0 = remote(own, own, plus)
        g1 = remote(own, own, minus)
        f0 = remote(rows_at(-1, 0), rows_at(-1, 0), plus)
        f1 = remote(rows_at(1, 1), rows_at(1, 1), minus)

        def one():
            g0.start()
            g1.start()

        def two():
            g0.wait_recv()
            f0.start()
            g1.wait_recv()
            f1.start()

        def three():
            f0.wait_recv()
            f1.wait_recv()

        return one, two, three

    small_gather = [gather(w, False, base_of[w], 64) for w in (0, 1)]
    large_gather = [gather(w, True, 0, 256) for w in (0, 1)]
    for w in (0, 1):
        lower, upper = second_stage[w][2]()
        begin = base_of[w] + small_of[w] * 64
        for part, value in ((0, lower), (1, upper)):
            rows = pl.ds(pl.multiple_of(begin + part * 32, 32), 32)
            na_v[rows, cols_of(w)] = (x_v[rows, cols_of(w)].astype(F32) + value).astype(BF16)
        small_gather[w][0]()

    a_two_own.wait()
    b_two_own.wait()
    for copy in a_two + b_two:
        copy.wait_recv()
    x_copies = []
    for k in range(1, 8):
        to = lax.rem(seq + k, 8)
        x_copies.append(remote(kvx_v.at[to // 2, lax.rem(to, 2)], kvout_hbm.at[seq], (to, ten)))
        x_copies[-1].start()
    x_own = local(kvx_v.at[xx, core], kvout_hbm.at[seq])

    for stage in small_gather:
        stage[1]()
    for w in (0, 1):
        small_gather[w][2]()
        large_gather[w][0]()
    for stage in large_gather:
        stage[1]()
    for stage in large_gather:
        stage[2]()
    out_copy = local(na_v, out_hbm)
    x_own.wait()
    for copy in x_copies:
        copy.wait_recv()
    out_copy.wait()
    for copy in pending:
        copy.wait_send()
    for k in (1, 2, 3):
        pl.when(xx + k < 4)(kv_out(seq, dev(x_=lax.rem(xx + k, 4)), k).wait_send)
    pl.when(core == 0)(kv_out(seq, twin, 0).wait_send)

    @pl.loop(0, xx)
    def _(step):
        base = 2 * (xx - 1 - step)
        kv_send(base + core, twin).wait_send()


def on_device(
    hidden_in,
    gain_attn,
    gain_mlp,
    w_qkv,
    w_attn_out,
    w_mlp_in,
    w_mlp_out,
    segment_ids,
    positions,
    kv_prefill,
    page_source,
):
    seq = lax.axis_index("seq")
    half = lax.rem(lax.axis_index("tensor"), 2)
    lane = jnp.arange(128, dtype=jnp.int32)[None, :]
    rot_dims = HD // 4
    freqs = 10000.0 ** (-((lane % (rot_dims // 2)).astype(F32) * 2.0 / rot_dims))
    angles = positions.astype(F32)[:, None] * freqs
    turns = (lane < rot_dims) & (half == 0)
    cosine = jnp.where(turns, jnp.cos(angles), 1.0)
    sine = jnp.where(turns, jnp.sin(angles) * jnp.where(lane < rot_dims // 2, -1.0, 1.0), 0.0)
    token_ids = seq * 1024 + jnp.arange(1024, dtype=jnp.int32)
    first = jnp.where(segment_ids == 0, 0, token_ids - positions)[None, :]
    vmem = pl.BlockSpec(memory_space=pltpu.VMEM)
    hbm = pl.BlockSpec(memory_space=pl.ANY)
    smem = pl.BlockSpec(memory_space=pltpu.SMEM)
    out, pages = pl.pallas_call(
        layer_kernel,
        name="layer",
        out_shape=(
            jax.ShapeDtypeStruct((1024, 2048), BF16),
            jax.ShapeDtypeStruct((8, 1024, 256), BF16),
        ),
        in_specs=[hbm, vmem, vmem, hbm, hbm, hbm, hbm, vmem, vmem, vmem, smem, hbm],
        out_specs=(hbm, hbm),
        scratch_shapes=[
            pltpu.VMEM((1024, 2048), BF16),
            pltpu.VMEM((1024, 2048), BF16),
            pltpu.VMEM((1024, 2048), BF16),
            pltpu.VMEM((2048, 384), BF16),
            pltpu.VMEM((2048, 512), BF16),
            pltpu.VMEM((512, 2048), BF16),
            pltpu.VMEM((256, 2048), BF16),
            pltpu.VMEM((1024, 512), BF16),
            pltpu.VMEM((1024, 2048), BF16),
            pltpu.VMEM((16, 1024, 128), BF16),
            pltpu.VMEM((16, 1024, 128), BF16),
            pltpu.VMEM((4, 4, 512, 128), BF16),
            pltpu.VMEM((4, 2, 512, 256), BF16),
            pltpu.VMEM((4, 2, 1024, 256), BF16),
            pltpu.VMEM((8, 2, 512, 256), BF16),
            pltpu.VMEM((2, 1024, 128), BF16),
            pltpu.VMEM((1024, 128), BF16),
            pltpu.VMEM((1024, 256), BF16),
            pltpu.VMEM((256, 1024), F32),
            pltpu.VMEM((8, 1024), F32),
            pltpu.VMEM((8, 1024), F32),
            pltpu.VMEM((8, 1024), F32),
            pltpu.VMEM((2, 2, 128, 1024), BF16),
            pltpu.VMEM((2, 2, 128, 1024), BF16),
            pltpu.VMEM((2, 2, 128, 1024), BF16),
            pltpu.VMEM((2, 2, 128, 1024), BF16),
            pltpu.VMEM((2, 256, 1024), BF16),
            pltpu.VMEM((2, 2, 32, 1024), BF16),
            pltpu.VMEM((2, 2, 32, 1024), BF16),
            pltpu.VMEM((2, 2, 32, 1024), BF16),
            pltpu.VMEM((2, 2, 32, 1024), BF16),
            pltpu.SemaphoreType.DMA((24,)),
            pltpu.SemaphoreType.DMA((80,)),
            pltpu.SemaphoreType.DMA((80,)),
            pltpu.SemaphoreType.DMA((12,)),
            pltpu.SemaphoreType.DMA((8,)),
        ],
        compiler_params=pltpu.CompilerParams(
            collective_id=0, has_side_effects=True, vmem_limit_bytes=67043328
        ),
    )(
        hidden_in,
        gain_attn[None, :],
        gain_mlp[None, :],
        w_qkv,
        w_attn_out,
        w_mlp_in,
        w_mlp_out,
        cosine,
        sine,
        first,
        page_source,
        kv_prefill.reshape(16, 1024, 128),
    )
    return (out, pages.reshape(8, 8, 2, 64, 256))


def solution(mesh):
    placed = (
        P("seq", None),
        P(),
        P(),
        P(None, None, "tensor"),
        P("tensor", None),
        P(None, "tensor"),
        P("tensor", None),
        P("seq"),
        P("seq"),
        P("seq", None, None, None, "tensor"),
        P(),
    )
    return jax.shard_map(
        on_device,
        mesh=mesh,
        in_specs=placed,
        out_specs=(P("seq", None), P("tensor", None, None, None, "seq")),
        check_vma=False,
    )
```

```python
import jax
import jax.numpy as jnp
import numpy as np
from jax import lax
from jax.experimental import pallas as pl
from jax.experimental.pallas import tpu as pltpu
from jax.sharding import PartitionSpec as P

MESH = pl.DeviceIdType.MESH
F32 = jnp.float32
BF16 = jnp.bfloat16
HD = 256
LOW = -1e30
MASKED = -3e30
TT = (((1,), (1,)), ((), ()))
FF = (((0,), (0,)), ((), ()))


def layer_kernel(
    x_hbm,
    ga_ref,
    gm_ref,
    wqkv_hbm,
    wo_hbm,
    wi_hbm,
    w2_hbm,
    freq_ref,
    seg_ref,
    pos_ref,
    psrc_ref,
    kv_hbm,
    out_hbm,
    kvout_hbm,
    x_v,
    na_v,
    nm_v,
    wcat_v,
    wi_v,
    w2_v,
    wo_v,
    hid_v,
    part_v,
    kvin_v,
    kvs_v,
    bufa_v,
    bufb_v,
    kvx_v,
    kvbuf_v,
    stage_v,
    qstage_v,
    q_v,
    acc_v,
    att_v,
    stat_v,
    mine_v,
    theirs_v,
    direct_v,
    relay_v,
    sums_v,
    merged_v,
    fold_v,
    direct2_v,
    relay2_v,
    sums2_v,
    merged2_v,
    cos_v,
    sin_v,
    first_v,
    lsem,
    ssem,
    rsem,
    kvs_sem,
    kvr_sem,
):
    seq = lax.axis_index("seq")
    ten = lax.axis_index("tensor")
    xx = seq // 2
    core = lax.rem(seq, 2)
    yy = ten // 4
    zz = lax.rem(ten, 4)
    half = lax.rem(ten, 2)
    zh = zz // 2

    def around(value, step):
        return lax.rem(value + step + 4, 4)

    def dev(x_=None, c_=None, y_=None, z_=None):
        x_ = xx if x_ is None else x_
        c_ = core if c_ is None else c_
        y_ = yy if y_ is None else y_
        z_ = zz if z_ is None else z_
        return (x_ * 2 + c_, y_ * 4 + z_)

    counter = [0]
    pending = []

    def remote(src, dst, device):
        index = counter[0]
        counter[0] += 1
        copy = pltpu.make_async_remote_copy(
            src_ref=src,
            dst_ref=dst,
            send_sem=ssem.at[index],
            recv_sem=rsem.at[index],
            device_id=device,
            device_id_type=MESH,
        )
        pending.append(copy)
        return copy

    local_count = [0]

    def local(src, dst):
        index = local_count[0]
        local_count[0] += 1
        copy = pltpu.make_async_copy(src, dst, lsem.at[index])
        copy.start()
        return copy

    barrier = pltpu.get_barrier_semaphore()
    peers = [dev(y_=around(yy, k)) for k in (1, 2, 3)]
    peers += [dev(z_=around(zz, k)) for k in (1, 2, 3)]
    peers += [(lax.rem(seq + k, 8), ten) for k in range(1, 8)]
    for peer in peers:
        pl.semaphore_signal(barrier, inc=1, device_id=peer, device_id_type=MESH)

    load_kv = local(kv_hbm, kvin_v)
    load_x = local(x_hbm, x_v)
    load_w = [local(wqkv_hbm.at[c], wcat_v.at[:, pl.ds(j * 128, 128)]) for j, c in ((0, 1), (1, 2), (2, 0))]
    load_wi = local(wi_hbm, wi_v)
    load_w2 = local(w2_hbm, w2_v)
    own_rows = pl.ds(pl.multiple_of(half * 128, 128), 128)
    load_wo = local(wo_hbm, wo_v.at[own_rows, :])

    load_kv.wait()

    @pl.loop(0, 16)
    def _(group):
        kvs_v[group] = kvin_v[lax.rem(psrc_ref[group * 8 + seq], 16)]

    pl.semaphore_wait(barrier, len(peers))

    partner = dev(z_=zz + 1 - 2 * half)
    twin = (seq + 1 - 2 * core, ten)

    half_rows = pl.ds(pl.multiple_of(half * 128 + core * 64, 64), 64)
    wo_cross = remote(wo_hbm.at[pl.ds(pl.multiple_of(core * 64, 64), 64)], wo_v.at[half_rows, :], partner)
    wo_cross.start()

    col_half = pl.ds(pl.multiple_of(half * 128, 128), 128)

    def low(part):
        return pl.ds(part * 256, 256)

    def high(part):
        return pl.ds(512 + part * 256, 256)

    def y_first(part):
        copies = [
            remote(kvs_v.at[pl.ds(around(yy, k) * 4, 4), low(part)], bufa_v.at[part, yy], dev(y_=around(yy, k)))
            for k in (1, 3, 2)
        ]
        for copy in copies:
            copy.start()
        return copies, [local(kvs_v.at[pl.ds(yy * 4, 4), low(part)], bufa_v.at[part, yy])]

    def then_z(part):
        copies = [
            remote(bufa_v.at[part, :, around(zz, k)], kvx_v.at[:, zh, low(part), col_half], dev(z_=around(zz, k)))
            for k in (1, 3, 2)
        ]
        for copy in copies:
            copy.start()
        return copies, [local(bufa_v.at[part, :, zz], kvx_v.at[:, zh, low(part), col_half])]

    def z_first(part):
        copies = [
            remote(
                kvs_v.at[y4 * 4 + around(zz, k), high(part)],
                bufb_v.at[part, y4, zh, :, col_half],
                dev(z_=around(zz, k)),
            )
            for k in (1, 3, 2)
            for y4 in range(4)
        ]
        for copy in copies:
            copy.start()
        own = [local(kvs_v.at[y4 * 4 + zz, high(part)], bufb_v.at[part, y4, zh, :, col_half]) for y4 in range(4)]
        return copies, own

    def then_y(part):
        copies = [
            remote(bufb_v.at[part, around(yy, k)], kvx_v.at[yy, :, high(part), :], dev(y_=around(yy, k)))
            for k in (1, 3, 2)
        ]
        for copy in copies:
            copy.start()
        return copies, [local(bufb_v.at[part, yy], kvx_v.at[yy, :, high(part), :])]

    def along_x(rows):
        copies = []
        for k in (1, 2, 7, 6, 3, 5, 4):
            to = lax.rem(seq + k, 8)
            copies.append(
                remote(kvx_v.at[to // 2, lax.rem(to, 2), rows], kvout_hbm.at[seq, rows], (to, ten))
            )
            copies[-1].start()
        return copies, [local(kvx_v.at[xx, core, rows], kvout_hbm.at[seq, rows])]

    def arrived(stage):
        copies, own = stage
        for copy in own:
            copy.wait()
        for copy in copies:
            copy.wait_recv()

    y_one = [y_first(0), y_first(1)]

    positions = pos_ref[...]
    angles = freq_ref[:, 0:1] * positions.astype(F32)
    turn = jnp.broadcast_to(half, (32, 1024)) == 0
    cosine = jnp.where(turn, jnp.cos(angles), 1.0)
    sine = jnp.where(turn, jnp.sin(angles), 0.0)
    cos_v[...] = jnp.concatenate([cosine, cosine, jnp.ones((64, 1024), F32)], axis=0).T
    sin_v[...] = jnp.concatenate([-sine, sine, jnp.zeros((64, 1024), F32)], axis=0).T
    tokens = seq * 1024 + lax.broadcasted_iota(jnp.int32, (1, 1024), 1)
    first_v[...] = jnp.where(seg_ref[...] == 0, 0, tokens - positions)

    load_x.wait()
    for copy in load_w:
        copy.wait()
    ga = ga_ref[...]
    gm = gm_ref[...]

    @pl.loop(0, 4)
    def _(step):
        start = lax.rem(step * 256 + (1 - half) * 512, 1024)
        rows = pl.ds(pl.multiple_of(start, 256), 256)
        values = x_v[rows, :].astype(F32)
        mean = jnp.mean(values, axis=-1, keepdims=True)
        centered = values - mean
        spread = jnp.mean(centered * centered, axis=-1, keepdims=True)
        normed = centered * lax.rsqrt(spread + 1e-05)
        na = (normed * ga).astype(BF16)
        na_v[rows, :] = na
        nm_v[rows, :] = (normed * gm).astype(BF16)
        kv = jnp.dot(na, wcat_v[:, 0:256], preferred_element_type=F32)
        q = jnp.dot(na, wcat_v[:, 256:384], preferred_element_type=F32)
        lanes = lax.broadcasted_iota(jnp.int32, (256, 128), 1)
        cosine = cos_v[rows, :]
        sine = sin_v[rows, :]

        def turned(values_in):
            other = jnp.where(lanes < 32, pltpu.roll(values_in, 96, 1), pltpu.roll(values_in, 32, 1))
            return values_in * cosine + other * sine

        stage_v[0, rows, :] = turned(kv[:, 0:128]).astype(BF16)
        stage_v[1, rows, :] = kv[:, 128:256].astype(BF16)
        qstage_v[rows, :] = (turned(q) * (HD**-0.5)).astype(BF16)

    own_keys = pl.ds(pl.multiple_of(half * 512, 512), 512)
    cross_keys = pl.ds(pl.multiple_of((1 - half) * 512, 512), 512)
    kv_cross = remote(stage_v.at[:, cross_keys], kvbuf_v.at[seq, :, :, col_half], partner)
    kv_cross.start()
    q_cross = remote(qstage_v, q_v.at[:, col_half], partner)
    q_cross.start()
    kv_own = local(stage_v.at[:, own_keys], kvbuf_v.at[seq, :, :, col_half])
    q_own = local(qstage_v, q_v.at[:, col_half])

    z_one = [z_first(0), z_first(1)]

    load_wi.wait()

    @pl.loop(0, 4)
    def _(step):
        rows = pl.ds(pl.multiple_of(step * 256, 256), 256)
        hidden = jnp.dot(nm_v[rows, :], wi_v[...], preferred_element_type=F32)
        hid_v[rows, :] = (0.5 * hidden * (1.0 + lax.erf(hidden * (0.5**0.5)))).astype(BF16)

    kv_own.wait()
    kv_cross.wait_recv()

    def kv_part(slot, part, device, index):
        return pltpu.make_async_remote_copy(
            src_ref=kvbuf_v.at[slot, part],
            dst_ref=kvbuf_v.at[slot, part],
            send_sem=kvs_sem.at[index],
            recv_sem=kvr_sem.at[slot, part],
            device_id=device,
            device_id_type=MESH,
        )

    def kv_twin(slot):
        return pltpu.make_async_remote_copy(
            src_ref=kvbuf_v.at[slot],
            dst_ref=kvbuf_v.at[slot],
            send_sem=kvs_sem.at[8 + slot],
            recv_sem=kvr_sem.at[slot, 2],
            device_id=twin,
            device_id_type=MESH,
        )

    def sends(copies):
        def start():
            for copy in copies:
                copy.start()

        def wait():
            for copy in copies:
                copy.wait_send()

        return start, wait

    chips = [dev(x_=k) for k in range(4)]
    own_out = [
        sends([kv_part(seq, 1, chips[3], 0), kv_part(seq, 0, chips[1], 1), kv_part(seq, 1, chips[1], 2), kv_part(seq, 0, chips[3], 3)]),
        sends([kv_part(seq, 1, chips[0], 0), kv_part(seq, 0, chips[2], 1), kv_part(seq, 1, chips[2], 2)]),
        sends([kv_part(seq, 0, chips[3], 0), kv_part(seq, 1, chips[3], 1)]),
    ]
    passed_on = [
        kv_part(2 + core, 1, chips[3], 4),
        kv_part(core, 0, chips[2], 4),
        kv_part(2 + core, 0, chips[3], 4),
        kv_part(core, 1, chips[2], 4),
    ]
    for k in range(3):
        pl.when(xx == k)(own_out[k][0])
    pl.when(core == 0)(kv_twin(seq).start)

    load_w2.wait()

    @pl.loop(0, 4)
    def _(step):
        rows = pl.ds(pl.multiple_of(step * 256, 256), 256)
        part_v[rows, :] = jnp.dot(hid_v[rows, :], w2_v[...], preferred_element_type=F32).astype(BF16)

    z_two = []
    for part in (0, 1):
        arrived(y_one[part])
        z_two.append(then_z(part))

    acc_v[...] = jnp.zeros_like(acc_v)
    stat_v[0:1, :] = jnp.full((1, 1024), LOW, F32)
    stat_v[1:2, :] = jnp.zeros((1, 1024), F32)

    def attend(slot):
        keys = kvbuf_v[slot, 0]
        vals = kvbuf_v[slot, 1]
        vals_t = vals.T
        key_ids = slot * 1024 + half * 512 + lax.broadcasted_iota(jnp.int32, (512, 1), 0)

        @pl.loop(0, 4)
        def _(step):
            cols = pl.ds(pl.multiple_of(step * 256, 256), 256)
            scores = lax.dot_general(keys, q_v[cols, :], TT, preferred_element_type=F32)
            query_ids = seq * 1024 + step * 256 + lax.broadcasted_iota(jnp.int32, (1, 256), 1)
            allowed = (key_ids >= first_v[:, cols]) & (key_ids <= query_ids)
            scores = jnp.where(allowed, scores, MASKED)
            old_max = stat_v[0:1, cols]
            new_max = jnp.maximum(old_max, jnp.max(scores, axis=0, keepdims=True))
            weights = jnp.exp(scores - new_max)
            keep = jnp.exp(old_max - new_max)
            stat_v[0:1, cols] = new_max
            stat_v[1:2, cols] = stat_v[1:2, cols] * keep + jnp.sum(weights, axis=0, keepdims=True)
            acc_v[:, cols] = acc_v[:, cols] * keep + jnp.dot(
                vals_t, weights.astype(BF16), preferred_element_type=F32
            )

    q_own.wait()
    q_cross.wait_recv()
    attend(seq)

    for k in range(4):

        @pl.when(xx == k)
        def _(k=k):
            passed_on[k].wait_recv()
            passed_on[k].start()

    arrived(z_one[0])
    y_two = [then_y(0)]

    @pl.when(core == 1)
    def _():
        kv_twin(seq - 1).wait_recv()
        attend(seq - 1)

    arrived(z_one[1])
    y_two.append(then_y(1))

    @pl.loop(0, xx)
    def _(step):
        base = 2 * (xx - 1 - step)
        pl.when(jnp.logical_or(step > 0, xx == 3))(kv_part(base + core, 0, twin, 0).wait_recv)
        pl.when(jnp.logical_or(base > 0, xx < 3))(kv_part(base + core, 1, twin, 0).wait_recv)
        kv_twin(base + core).start()
        attend(base + core)
        kv_twin(base + 1 - core).wait_recv()
        attend(base + 1 - core)

    mine_v[...] = stat_v[...]
    stat_cross = remote(mine_v, theirs_v, partner)
    stat_cross.start()
    load_wo.wait()
    wo_cross.wait_recv()
    wo_twin = remote(wo_v.at[pl.ds(pl.multiple_of((1 - half) * 128 + core * 64, 64), 64), :],
                     wo_v.at[pl.ds(pl.multiple_of((1 - half) * 128 + core * 64, 64), 64), :], twin)
    wo_twin.start()
    wo_twin.wait_recv()
    stat_cross.wait_recv()
    top = jnp.maximum(stat_v[0:1, :], theirs_v[0:1, :])
    mine = jnp.exp(stat_v[0:1, :] - top)
    total = stat_v[1:2, :] * mine + theirs_v[1:2, :] * jnp.exp(theirs_v[0:1, :] - top)
    stat_v[0:1, :] = mine / total

    att_v[...] = (acc_v[...] * stat_v[0:1, :]).astype(BF16)

    def project(group):
        cols = cols_of(group)

        @pl.loop(0, 4)
        def _(step):
            rows = pl.ds(pl.multiple_of(step * 256, 256), 256)
            summed = lax.dot_general(att_v[:, rows], wo_v[:, cols], FF, preferred_element_type=F32)
            part_v[rows, cols] = (part_v[rows, cols].astype(F32) + summed).astype(BF16)

    def cols_of(which):
        return pl.ds(which * 512, 512)

    def axis_dev(which, step, first):
        along_y = (which % 2 == 0) == first
        return dev(y_=around(yy, step)) if along_y else dev(z_=around(zz, step))

    def scatter(which, first, source, size, direct, relay, sums, merged):
        pos = yy if (which % 2 == 0) == first else zz
        hs = size // 2

        def piece(step, part):
            begin = around(pos, step) * size + part * hs
            return source(pl.ds(pl.multiple_of(begin, hs), hs))

        plus = axis_dev(which, 1, first)
        minus = axis_dev(which, -1, first)
        r0 = remote(piece(2, 0), relay.at[which, 0], plus)
        r1 = remote(piece(2, 1), relay.at[which, 1], minus)
        d0 = remote(piece(1, 1), direct.at[which, 0], plus)
        d1 = remote(piece(-1, 0), direct.at[which, 1], minus)
        m0 = remote(sums.at[which, 0], merged.at[which, 0], plus)
        m1 = remote(sums.at[which, 1], merged.at[which, 1], minus)

        def one():
            for copy in (r0, r1, d0, d1):
                copy.start()

        def two():
            r0.wait_recv()
            sums[which, 0] = (piece(1, 0)[...].astype(F32) + relay[which, 0].astype(F32)).astype(BF16)
            m0.start()
            r1.wait_recv()
            sums[which, 1] = (piece(-1, 1)[...].astype(F32) + relay[which, 1].astype(F32)).astype(BF16)
            m1.start()

        def three():
            d0.wait_recv()
            d1.wait_recv()
            m0.wait_recv()
            m1.wait_recv()
            lower = piece(0, 0)[...].astype(F32) + direct[which, 1].astype(F32) + merged[which, 0].astype(F32)
            upper = piece(0, 1)[...].astype(F32) + direct[which, 0].astype(F32) + merged[which, 1].astype(F32)
            return lower, upper

        return one, two, three

    groups = range(4)
    first_stage = [
        scatter(w, True, lambda rows, w=w: part_v.at[rows, cols_of(w)], 256, direct_v, relay_v, sums_v, merged_v)
        for w in groups
    ]
    second_stage = [
        scatter(w, False, lambda rows, w=w: fold_v.at[w, rows], 64, direct2_v, relay2_v, sums2_v, merged2_v)
        for w in groups
    ]
    for w in groups:
        project(w)
        first_stage[w][0]()
    arrived(y_two[0])
    x_three = [along_x(high(0))]
    for w in groups:
        first_stage[w][1]()
    arrived(z_two[0])
    x_three.append(along_x(low(0)))
    for w in groups:
        lower, upper = first_stage[w][2]()
        fold_v[w, 0:128] = lower.astype(BF16)
        fold_v[w, 128:256] = upper.astype(BF16)
        second_stage[w][0]()
    arrived(y_two[1])
    x_three.append(along_x(high(1)))
    arrived(z_two[1])
    x_three.append(along_x(low(1)))
    for w in groups:
        second_stage[w][1]()

    base_of = (yy * 256, zz * 256) * 2
    small_of = (zz, yy) * 2

    def gather(which, first, base, size):
        pos = yy if (which % 2 == 0) == first else zz
        hs = size // 2

        def rows_at(step, part=None):
            begin = base + around(pos, step) * size
            if part is None:
                return na_v.at[pl.ds(pl.multiple_of(begin, size), size), cols_of(which)]
            return na_v.at[pl.ds(pl.multiple_of(begin + part * hs, hs), hs), cols_of(which)]

        plus = axis_dev(which, 1, first)
        minus = axis_dev(which, -1, first)
        own = rows_at(0)
        g0 = remote(own, own, plus)
        g1 = remote(own, own, minus)
        f0 = remote(rows_at(-1, 0), rows_at(-1, 0), plus)
        f1 = remote(rows_at(1, 1), rows_at(1, 1), minus)

        def one():
            g0.start()
            g1.start()

        def two():
            g0.wait_recv()
            f0.start()
            g1.wait_recv()
            f1.start()

        def three():
            f0.wait_recv()
            f1.wait_recv()

        return one, two, three

    small_gather = [gather(w, False, base_of[w], 64) for w in groups]
    large_gather = [gather(w, True, 0, 256) for w in groups]
    for w in groups:
        lower, upper = second_stage[w][2]()
        begin = base_of[w] + small_of[w] * 64
        for part, value in ((0, lower), (1, upper)):
            rows = pl.ds(pl.multiple_of(begin + part * 32, 32), 32)
            na_v[rows, cols_of(w)] = (x_v[rows, cols_of(w)].astype(F32) + value).astype(BF16)
        small_gather[w][0]()
    for w in groups:
        small_gather[w][1]()
    for w in groups:
        small_gather[w][2]()
        large_gather[w][0]()
    for w in groups:
        large_gather[w][1]()
    for w in groups:
        large_gather[w][2]()
    out_copies = [local(na_v.at[pl.ds(k * 256, 256)], out_hbm.at[k]) for k in range(4)]
    for stage in x_three:
        arrived(stage)
    for copy in out_copies:
        copy.wait()
    for copy in pending:
        copy.wait_send()
    for k in range(3):
        pl.when(xx == k)(own_out[k][1])
    for k in range(4):
        pl.when(xx == k)(passed_on[k].wait_send)
    pl.when(core == 0)(kv_twin(seq).wait_send)

    @pl.loop(0, xx)
    def _(step):
        base = 2 * (xx - 1 - step)
        kv_twin(base + core).wait_send()


def on_device(
    hidden_in,
    gain_attn,
    gain_mlp,
    w_qkv,
    w_attn_out,
    w_mlp_in,
    w_mlp_out,
    segment_ids,
    positions,
    kv_prefill,
    page_source,
):
    rot_dims = HD // 4
    powers = np.arange(rot_dims // 2, dtype=np.float32) * np.float32(2.0) / np.float32(rot_dims)
    freqs = np.power(np.float32(10000.0), -powers).astype(np.float32)
    freqs = jnp.asarray(np.broadcast_to(freqs[:, None], (rot_dims // 2, 128)))
    vmem = pl.BlockSpec(memory_space=pltpu.VMEM)
    hbm = pl.BlockSpec(memory_space=pl.ANY)
    smem = pl.BlockSpec(memory_space=pltpu.SMEM)
    out, pages = pl.pallas_call(
        layer_kernel,
        name="layer",
        out_shape=(
            jax.ShapeDtypeStruct((4, 256, 2048), BF16),
            jax.ShapeDtypeStruct((8, 1024, 256), BF16),
        ),
        in_specs=[hbm, vmem, vmem, hbm, hbm, hbm, hbm, vmem, vmem, vmem, smem, hbm],
        out_specs=(hbm, hbm),
        scratch_shapes=[
            pltpu.VMEM((1024, 2048), BF16),
            pltpu.VMEM((1024, 2048), BF16),
            pltpu.VMEM((1024, 2048), BF16),
            pltpu.VMEM((2048, 384), BF16),
            pltpu.VMEM((2048, 512), BF16),
            pltpu.VMEM((512, 2048), BF16),
            pltpu.VMEM((256, 2048), BF16),
            pltpu.VMEM((1024, 512), BF16),
            pltpu.VMEM((1024, 2048), BF16),
            pltpu.VMEM((16, 1024, 128), BF16),
            pltpu.VMEM((16, 1024, 128), BF16),
            pltpu.VMEM((2, 4, 4, 256, 128), BF16),
            pltpu.VMEM((2, 4, 2, 256, 256), BF16),
            pltpu.VMEM((4, 2, 1024, 256), BF16),
            pltpu.VMEM((8, 2, 512, 256), BF16),
            pltpu.VMEM((2, 1024, 128), BF16),
            pltpu.VMEM((1024, 128), BF16),
            pltpu.VMEM((1024, 256), BF16),
            pltpu.VMEM((256, 1024), F32),
            pltpu.VMEM((256, 1024), BF16),
            pltpu.VMEM((8, 1024), F32),
            pltpu.VMEM((8, 1024), F32),
            pltpu.VMEM((8, 1024), F32),
            pltpu.VMEM((4, 2, 128, 512), BF16),
            pltpu.VMEM((4, 2, 128, 512), BF16),
            pltpu.VMEM((4, 2, 128, 512), BF16),
            pltpu.VMEM((4, 2, 128, 512), BF16),
            pltpu.VMEM((4, 256, 512), BF16),
            pltpu.VMEM((4, 2, 32, 512), BF16),
            pltpu.VMEM((4, 2, 32, 512), BF16),
            pltpu.VMEM((4, 2, 32, 512), BF16),
            pltpu.VMEM((4, 2, 32, 512), BF16),
            pltpu.VMEM((1024, 128), F32),
            pltpu.VMEM((1024, 128), F32),
            pltpu.VMEM((1, 1024), jnp.int32),
            pltpu.SemaphoreType.DMA((48,)),
            pltpu.SemaphoreType.DMA((160,)),
            pltpu.SemaphoreType.DMA((160,)),
            pltpu.SemaphoreType.DMA((16,)),
            pltpu.SemaphoreType.DMA((8, 3)),
        ],
        compiler_params=pltpu.CompilerParams(
            collective_id=0, has_side_effects=True, vmem_limit_bytes=67043328
        ),
    )(
        hidden_in,
        gain_attn[None, :],
        gain_mlp[None, :],
        w_qkv,
        w_attn_out,
        w_mlp_in,
        w_mlp_out,
        freqs,
        segment_ids[None, :],
        positions[None, :],
        page_source,
        kv_prefill.reshape(16, 1024, 128),
    )
    return (out.reshape(1024, 2048), pages.reshape(8, 8, 2, 64, 256))


def solution(mesh):
    placed = (
        P("seq", None),
        P(),
        P(),
        P(None, None, "tensor"),
        P("tensor", None),
        P(None, "tensor"),
        P("tensor", None),
        P("seq"),
        P("seq"),
        P("seq", None, None, None, "tensor"),
        P(),
    )
    return jax.shard_map(
        on_device,
        mesh=mesh,
        in_specs=placed,
        out_specs=(P("seq", None), P("tensor", None, None, None, "seq")),
        check_vma=False,
    )
```

```python
import jax
import jax.numpy as jnp
import numpy as np
from jax import lax
from jax.experimental import pallas as pl
from jax.experimental.pallas import tpu as pltpu
from jax.sharding import PartitionSpec as P

MESH = pl.DeviceIdType.MESH
F32 = jnp.float32
BF16 = jnp.bfloat16
HD = 256
LOW = -1e30
MASKED = -3e30
TT = (((1,), (1,)), ((), ()))
FF = (((0,), (0,)), ((), ()))


def layer_kernel(
    x_hbm,
    ga_ref,
    gm_ref,
    wqkv_hbm,
    wo_hbm,
    wi_hbm,
    w2_hbm,
    freq_ref,
    seg_ref,
    pos_ref,
    psrc_ref,
    kv_hbm,
    out_hbm,
    kvout_hbm,
    x_v,
    na_v,
    wcat_v,
    wi_v,
    w2_v,
    wo_v,
    hid_v,
    part_v,
    kvin_v,
    kvs_v,
    bufa_v,
    bufb_v,
    kvx_v,
    kvbuf_v,
    stage_v,
    q_v,
    acc_v,
    att_v,
    stat_v,
    mine_v,
    theirs_v,
    direct_v,
    relay_v,
    sums_v,
    merged_v,
    fold_v,
    direct2_v,
    relay2_v,
    sums2_v,
    merged2_v,
    cos_v,
    sin_v,
    first_v,
    lsem,
    ssem,
    rsem,
    kvs_sem,
    kvr_sem,
):
    seq = lax.axis_index("seq")
    ten = lax.axis_index("tensor")
    xx = seq // 2
    core = lax.rem(seq, 2)
    yy = ten // 4
    zz = lax.rem(ten, 4)
    half = lax.rem(ten, 2)
    zh = zz // 2

    def around(value, step):
        return lax.rem(value + step + 4, 4)

    def dev(x_=None, c_=None, y_=None, z_=None):
        x_ = xx if x_ is None else x_
        c_ = core if c_ is None else c_
        y_ = yy if y_ is None else y_
        z_ = zz if z_ is None else z_
        return (x_ * 2 + c_, y_ * 4 + z_)

    counter = [0]
    pending = []

    def remote(src, dst, device):
        index = counter[0]
        counter[0] += 1
        copy = pltpu.make_async_remote_copy(
            src_ref=src,
            dst_ref=dst,
            send_sem=ssem.at[index],
            recv_sem=rsem.at[index],
            device_id=device,
            device_id_type=MESH,
        )
        pending.append(copy)
        return copy

    local_count = [0]

    def local(src, dst):
        index = local_count[0]
        local_count[0] += 1
        copy = pltpu.make_async_copy(src, dst, lsem.at[index])
        copy.start()
        return copy

    barrier = pltpu.get_barrier_semaphore()
    peers = [dev(y_=around(yy, k)) for k in (1, 2, 3)]
    peers += [dev(z_=around(zz, k)) for k in (1, 2, 3)]
    peers += [(lax.rem(seq + k, 8), ten) for k in range(1, 8)]
    for peer in peers:
        pl.semaphore_signal(barrier, inc=1, device_id=peer, device_id_type=MESH)

    load_kv = local(kv_hbm, kvin_v)
    load_x = local(x_hbm, x_v)
    q_cols = pl.ds(pl.multiple_of(256 + half * 128, 128), 128)
    load_w = [local(wqkv_hbm.at[1], wcat_v.at[:, 0:128]), local(wqkv_hbm.at[2], wcat_v.at[:, 128:256])]
    load_w.append(local(wqkv_hbm.at[0], wcat_v.at[:, q_cols]))
    load_wi = local(wi_hbm, wi_v)
    load_w2 = local(w2_hbm, w2_v)
    own_rows = pl.ds(pl.multiple_of(half * 128, 128), 128)
    load_wo = local(wo_hbm, wo_v.at[own_rows, :])

    load_kv.wait()

    @pl.loop(0, 16)
    def _(group):
        kvs_v[group] = kvin_v[lax.rem(psrc_ref[group * 8 + seq], 16)]

    pl.semaphore_wait(barrier, len(peers))

    partner = dev(z_=zz + 1 - 2 * half)
    twin = (seq + 1 - 2 * core, ten)

    wo_piece = pl.ds(pl.multiple_of(seq * 16, 16), 16)
    wq_piece = pl.ds(pl.multiple_of(seq * 256, 256), 256)
    pair_weights = [
        remote(wo_hbm.at[wo_piece], wo_v.at[pl.ds(pl.multiple_of(half * 128 + seq * 16, 16), 16)], partner),
        remote(wqkv_hbm.at[0, wq_piece], wcat_v.at[wq_piece, q_cols], partner),
    ]
    for copy in pair_weights:
        copy.start()
    wo_here = wo_v.at[pl.ds(pl.multiple_of((1 - half) * 128 + seq * 16, 16), 16)]
    wq_here = wcat_v.at[wq_piece, pl.ds(pl.multiple_of(256 + (1 - half) * 128, 128), 128)]
    seq_weights = [
        remote(piece, piece, (lax.rem(seq + k, 8), ten)) for piece in (wq_here, wo_here) for k in (1, 2, 7, 6, 3, 5, 4)
    ]

    col_half = pl.ds(pl.multiple_of(half * 128, 128), 128)

    def low(part):
        return pl.ds(part * 256, 256)

    def high(part):
        return pl.ds(512 + part * 256, 256)

    def y_first(part):
        copies = [
            remote(kvs_v.at[pl.ds(around(yy, k) * 4, 4), low(part)], bufa_v.at[part, yy], dev(y_=around(yy, k)))
            for k in (1, 3, 2)
        ]
        for copy in copies:
            copy.start()
        return copies, [local(kvs_v.at[pl.ds(yy * 4, 4), low(part)], bufa_v.at[part, yy])]

    def then_z(part):
        copies = [
            remote(bufa_v.at[part, :, around(zz, k)], kvx_v.at[:, zh, low(part), col_half], dev(z_=around(zz, k)))
            for k in (1, 3, 2)
        ]
        for copy in copies:
            copy.start()
        return copies, [local(bufa_v.at[part, :, zz], kvx_v.at[:, zh, low(part), col_half])]

    away = 2 * half - 1

    def z_first(part):
        return [
            [
                remote(
                    kvs_v.at[y4 * 4 + around(zz, k), high(part)],
                    bufb_v.at[part, y4, zh, :, col_half],
                    dev(z_=around(zz, k)),
                )
                for y4 in range(4)
            ]
            for k in (away, -away, 2)
        ]

    def z_own(part):
        return [local(kvs_v.at[y4 * 4 + zz, high(part)], bufb_v.at[part, y4, zh, :, col_half]) for y4 in range(4)]

    def then_y(part):
        copies = [
            remote(bufb_v.at[part, around(yy, k)], kvx_v.at[yy, :, high(part), :], dev(y_=around(yy, k)))
            for k in (1, 3, 2)
        ]
        for copy in copies:
            copy.start()
        return copies, [local(bufb_v.at[part, yy], kvx_v.at[yy, :, high(part), :])]

    def along_x(rows):
        copies = []
        for k in (1, 2, 7, 6, 3, 5, 4):
            to = lax.rem(seq + k, 8)
            copies.append(
                remote(kvx_v.at[to // 2, lax.rem(to, 2), rows], kvout_hbm.at[seq, rows], (to, ten))
            )
            copies[-1].start()
        return copies, [local(kvx_v.at[xx, core, rows], kvout_hbm.at[seq, rows])]

    def arrived(stage):
        copies, own = stage
        for copy in own:
            copy.wait()
        for copy in copies:
            copy.wait_recv()

    y_one = [y_first(0), y_first(1)]
    z_sends = [z_first(0), z_first(1)]
    for part in (0, 1):
        for copy in z_sends[part][0]:
            copy.start()

    positions = pos_ref[...]
    freqs = jnp.broadcast_to(freq_ref[...], (128, 128)).T[0:32, 0:1]
    angles = freqs * positions.astype(F32)
    cosine = jnp.cos(angles)
    sine = jnp.sin(angles)
    cos_v[...] = jnp.concatenate([cosine, cosine, jnp.ones((64, 1024), F32)], axis=0).T
    sin_v[...] = jnp.concatenate([-sine, sine, jnp.zeros((64, 1024), F32)], axis=0).T
    tokens = seq * 1024 + lax.broadcasted_iota(jnp.int32, (1, 1024), 1)
    first_v[...] = jnp.where(seg_ref[...] == 0, 0, tokens - positions)

    load_x.wait()
    for copy in load_w:
        copy.wait()
    ga = ga_ref[...]
    gm = gm_ref[...]

    def normed_rows(rows):
        values = x_v[rows, :].astype(F32)
        mean = jnp.mean(values, axis=-1, keepdims=True)
        centered = values - mean
        spread = jnp.mean(centered * centered, axis=-1, keepdims=True)
        return centered * lax.rsqrt(spread + 1e-05)

    def turned(values_in, rows):
        lanes = lax.broadcasted_iota(jnp.int32, (256, 128), 1)
        other = jnp.where(lanes < 32, pltpu.roll(values_in, 96, 1), pltpu.roll(values_in, 32, 1))
        return values_in * cos_v[rows, :] + other * sin_v[rows, :]

    def keys_values(first_step):
        @pl.loop(first_step, first_step + 2)
        def _(step):
            start = lax.rem(step * 256 + (1 - half) * 512, 1024)
            rows = pl.ds(pl.multiple_of(start, 256), 256)
            na = (normed_rows(rows) * ga).astype(BF16)
            na_v[rows, :] = na
            kv = jnp.dot(na, wcat_v[:, 0:256], preferred_element_type=F32)
            keys = kv[:, 0:128]
            keys = jnp.where(jnp.broadcast_to(half, (256, 128)) == 0, turned(keys, rows), keys)
            stage_v[0, rows, :] = keys.astype(BF16)
            stage_v[1, rows, :] = kv[:, 128:256].astype(BF16)

    keys_values(0)
    own_keys = pl.ds(pl.multiple_of(half * 512, 512), 512)
    cross_keys = pl.ds(pl.multiple_of((1 - half) * 512, 512), 512)
    kv_cross = remote(stage_v.at[:, cross_keys], kvbuf_v.at[seq, :, :, col_half], partner)
    kv_cross.start()
    for copy in pair_weights:
        copy.wait_recv()
    for copy in seq_weights:
        copy.start()
    z_one = []
    for part in (0, 1):
        for copies in z_sends[part][1:]:
            for copy in copies:
                copy.start()
        z_one.append(([copy for copies in z_sends[part] for copy in copies], z_own(part)))
    keys_values(2)
    kv_own = local(stage_v.at[:, own_keys], kvbuf_v.at[seq, :, :, col_half])

    load_wi.wait()

    def mlp_in(first_step):
        @pl.loop(first_step, first_step + 2)
        def _(step):
            rows = pl.ds(pl.multiple_of(step * 256, 256), 256)
            nm = (normed_rows(rows) * gm).astype(BF16)
            hidden = jnp.dot(nm, wi_v[...], preferred_element_type=F32)
            hid_v[rows, :] = (0.5 * hidden * (1.0 + lax.erf(hidden * (0.5**0.5)))).astype(BF16)

    mlp_in(0)

    kv_own.wait()
    kv_cross.wait_recv()

    def kv_part(slot, part, device, index):
        return pltpu.make_async_remote_copy(
            src_ref=kvbuf_v.at[slot, part],
            dst_ref=kvbuf_v.at[slot, part],
            send_sem=kvs_sem.at[index],
            recv_sem=kvr_sem.at[slot, part],
            device_id=device,
            device_id_type=MESH,
        )

    def kv_twin(slot):
        return pltpu.make_async_remote_copy(
            src_ref=kvbuf_v.at[slot],
            dst_ref=kvbuf_v.at[slot],
            send_sem=kvs_sem.at[8 + slot],
            recv_sem=kvr_sem.at[slot, 2],
            device_id=twin,
            device_id_type=MESH,
        )

    def sends(copies):
        def start():
            for copy in copies:
                copy.start()

        def wait():
            for copy in copies:
                copy.wait_send()

        return start, wait

    chips = [dev(x_=k) for k in range(4)]
    own_out = [
        sends([kv_part(seq, 1, chips[3], 0), kv_part(seq, 0, chips[1], 1), kv_part(seq, 1, chips[1], 2), kv_part(seq, 0, chips[3], 3)]),
        sends([kv_part(seq, 1, chips[0], 0), kv_part(seq, 0, chips[2], 1), kv_part(seq, 1, chips[2], 2)]),
        sends([kv_part(seq, 0, chips[3], 0), kv_part(seq, 1, chips[3], 1)]),
    ]
    passed_on = [
        kv_part(2 + core, 1, chips[3], 4),
        kv_part(core, 0, chips[2], 4),
        kv_part(2 + core, 0, chips[3], 4),
        kv_part(core, 1, chips[2], 4),
    ]
    for k in range(3):
        pl.when(xx == k)(own_out[k][0])
    pl.when(core == 0)(kv_twin(seq).start)

    mlp_in(2)

    for copy in seq_weights[:7]:
        copy.wait_recv()

    @pl.loop(0, 4)
    def _(step):
        rows = pl.ds(pl.multiple_of(step * 256, 256), 256)
        q = jnp.dot(na_v[rows, :], wcat_v[:, 256:512], preferred_element_type=F32) * (HD**-0.5)
        q_v[rows, 0:128] = turned(q[:, 0:128], rows).astype(BF16)
        q_v[rows, 128:256] = q[:, 128:256].astype(BF16)

    load_w2.wait()

    @pl.loop(0, 4)
    def _(step):
        rows = pl.ds(pl.multiple_of(step * 256, 256), 256)
        part_v[rows, :] = jnp.dot(hid_v[rows, :], w2_v[...], preferred_element_type=F32).astype(BF16)

    z_two = []
    for part in (0, 1):
        arrived(y_one[part])
        z_two.append(then_z(part))

    acc_v[...] = jnp.zeros_like(acc_v)
    stat_v[0:1, :] = jnp.full((1, 1024), LOW, F32)
    stat_v[1:2, :] = jnp.zeros((1, 1024), F32)

    def attend(slot):
        keys = kvbuf_v[slot, 0]
        vals = kvbuf_v[slot, 1]
        vals_t = vals.T
        key_ids = slot * 1024 + half * 512 + lax.broadcasted_iota(jnp.int32, (512, 1), 0)

        @pl.loop(0, 4)
        def _(step):
            cols = pl.ds(pl.multiple_of(step * 256, 256), 256)
            scores = lax.dot_general(keys, q_v[cols, :], TT, preferred_element_type=F32)
            query_ids = seq * 1024 + step * 256 + lax.broadcasted_iota(jnp.int32, (1, 256), 1)
            allowed = (key_ids >= first_v[:, cols]) & (key_ids <= query_ids)
            scores = jnp.where(allowed, scores, MASKED)
            old_max = stat_v[0:1, cols]
            new_max = jnp.maximum(old_max, jnp.max(scores, axis=0, keepdims=True))
            weights = jnp.exp(scores - new_max)
            keep = jnp.exp(old_max - new_max)
            stat_v[0:1, cols] = new_max
            stat_v[1:2, cols] = stat_v[1:2, cols] * keep + jnp.sum(weights, axis=0, keepdims=True)
            acc_v[:, cols] = acc_v[:, cols] * keep + jnp.dot(
                vals_t, weights.astype(BF16), preferred_element_type=F32
            )

    attend(seq)

    for k in range(4):

        @pl.when(xx == k)
        def _(k=k):
            passed_on[k].wait_recv()
            passed_on[k].start()

    arrived(z_one[0])
    y_two = [then_y(0)]

    @pl.when(core == 1)
    def _():
        kv_twin(seq - 1).wait_recv()
        attend(seq - 1)

    arrived(z_one[1])
    y_two.append(then_y(1))

    @pl.loop(0, xx)
    def _(step):
        base = 2 * (xx - 1 - step)
        pl.when(jnp.logical_or(step > 0, xx == 3))(kv_part(base + core, 0, twin, 0).wait_recv)
        pl.when(jnp.logical_or(base > 0, xx < 3))(kv_part(base + core, 1, twin, 0).wait_recv)
        kv_twin(base + core).start()
        attend(base + core)
        kv_twin(base + 1 - core).wait_recv()
        attend(base + 1 - core)

    mine_v[...] = stat_v[...]
    stat_cross = remote(mine_v, theirs_v, partner)
    stat_cross.start()
    load_wo.wait()
    for copy in seq_weights[7:]:
        copy.wait_recv()
    stat_cross.wait_recv()
    top = jnp.maximum(stat_v[0:1, :], theirs_v[0:1, :])
    mine = jnp.exp(stat_v[0:1, :] - top)
    total = stat_v[1:2, :] * mine + theirs_v[1:2, :] * jnp.exp(theirs_v[0:1, :] - top)
    stat_v[0:1, :] = mine / total

    att_v[...] = (acc_v[...] * stat_v[0:1, :]).astype(BF16)

    def project(group):
        cols = cols_of(group)

        @pl.loop(0, 4)
        def _(step):
            rows = pl.ds(pl.multiple_of(step * 256, 256), 256)
            summed = lax.dot_general(att_v[:, rows], wo_v[:, cols], FF, preferred_element_type=F32)
            part_v[rows, cols] = (part_v[rows, cols].astype(F32) + summed).astype(BF16)

    widths = (640, 384, 512, 512)
    starts = (0, 640, 1024, 1536)

    def cols_of(which):
        return pl.ds(starts[which], widths[which])

    def axis_dev(which, step, first):
        along_y = (which % 2 == 0) == first
        return dev(y_=around(yy, step)) if along_y else dev(z_=around(zz, step))

    def scatter(which, first, source, size, direct, relay, sums, merged):
        pos = yy if (which % 2 == 0) == first else zz
        hs = size // 2
        wide = pl.ds(0, widths[which])
        direct, relay, sums, merged = (
            [buf.at[which, k, :, wide] for k in (0, 1)] for buf in (direct, relay, sums, merged)
        )

        def piece(step, part):
            begin = around(pos, step) * size + part * hs
            return source(pl.ds(pl.multiple_of(begin, hs), hs))

        plus = axis_dev(which, 1, first)
        minus = axis_dev(which, -1, first)
        r0 = remote(piece(2, 0), relay[0], plus)
        r1 = remote(piece(2, 1), relay[1], minus)
        d0 = remote(piece(1, 1), direct[0], plus)
        d1 = remote(piece(-1, 0), direct[1], minus)
        m0 = remote(sums[0], merged[0], plus)
        m1 = remote(sums[1], merged[1], minus)

        def one():
            for copy in (r0, r1, d0, d1):
                copy.start()

        def two():
            r0.wait_recv()
            sums[0][...] = (piece(1, 0)[...].astype(F32) + relay[0][...].astype(F32)).astype(BF16)
            m0.start()
            r1.wait_recv()
            sums[1][...] = (piece(-1, 1)[...].astype(F32) + relay[1][...].astype(F32)).astype(BF16)
            m1.start()

        def three():
            d0.wait_recv()
            d1.wait_recv()
            m0.wait_recv()
            m1.wait_recv()
            lower = piece(0, 0)[...].astype(F32) + direct[1][...].astype(F32) + merged[0][...].astype(F32)
            upper = piece(0, 1)[...].astype(F32) + direct[0][...].astype(F32) + merged[1][...].astype(F32)
            return lower, upper

        return one, two, three

    groups = range(4)
    first_stage = [
        scatter(w, True, lambda rows, w=w: part_v.at[rows, cols_of(w)], 256, direct_v, relay_v, sums_v, merged_v)
        for w in groups
    ]
    second_stage = [
        scatter(w, False, lambda rows, w=w: fold_v.at[w, rows, pl.ds(0, widths[w])], 64, direct2_v, relay2_v, sums2_v, merged2_v)
        for w in groups
    ]
    for w in groups:
        project(w)
        first_stage[w][0]()
    arrived(y_two[0])
    x_three = [along_x(high(0))]
    for w in groups:
        first_stage[w][1]()
    arrived(z_two[0])
    x_three.append(along_x(low(0)))
    for w in groups:
        lower, upper = first_stage[w][2]()
        fold_v[w, 0:128, 0 : widths[w]] = lower.astype(BF16)
        fold_v[w, 128:256, 0 : widths[w]] = upper.astype(BF16)
        second_stage[w][0]()
    arrived(y_two[1])
    x_three.append(along_x(high(1)))
    arrived(z_two[1])
    x_three.append(along_x(low(1)))
    for w in groups:
        second_stage[w][1]()

    base_of = (yy * 256, zz * 256) * 2
    small_of = (zz, yy) * 2

    def gather(which, first, base, size):
        pos = yy if (which % 2 == 0) == first else zz
        hs = size // 2

        def rows_at(step, part=None):
            begin = base + around(pos, step) * size
            if part is None:
                return na_v.at[pl.ds(pl.multiple_of(begin, size), size), cols_of(which)]
            return na_v.at[pl.ds(pl.multiple_of(begin + part * hs, hs), hs), cols_of(which)]

        plus = axis_dev(which, 1, first)
        minus = axis_dev(which, -1, first)
        own = rows_at(0)
        g0 = remote(own, own, plus)
        g1 = remote(own, own, minus)
        f0 = remote(rows_at(-1, 0), rows_at(-1, 0), plus)
        f1 = remote(rows_at(1, 1), rows_at(1, 1), minus)

        def one():
            g0.start()
            g1.start()

        def two():
            g0.wait_recv()
            f0.start()
            g1.wait_recv()
            f1.start()

        def three():
            f0.wait_recv()
            f1.wait_recv()

        return one, two, three

    small_gather = [gather(w, False, base_of[w], 64) for w in groups]
    large_gather = [gather(w, True, 0, 256) for w in groups]
    for w in groups:
        lower, upper = second_stage[w][2]()
        begin = base_of[w] + small_of[w] * 64
        for part, value in ((0, lower), (1, upper)):
            rows = pl.ds(pl.multiple_of(begin + part * 32, 32), 32)
            na_v[rows, cols_of(w)] = (x_v[rows, cols_of(w)].astype(F32) + value).astype(BF16)
        small_gather[w][0]()
    for w in groups:
        small_gather[w][1]()
    for w in groups:
        small_gather[w][2]()
        large_gather[w][0]()
    for w in groups:
        large_gather[w][1]()
    for w in groups:
        large_gather[w][2]()
    out_copies = [local(na_v.at[pl.ds(k * 256, 256)], out_hbm.at[k]) for k in range(4)]
    for stage in x_three:
        arrived(stage)
    for copy in out_copies:
        copy.wait()
    for copy in pending:
        copy.wait_send()
    for k in range(3):
        pl.when(xx == k)(own_out[k][1])
    for k in range(4):
        pl.when(xx == k)(passed_on[k].wait_send)
    pl.when(core == 0)(kv_twin(seq).wait_send)

    @pl.loop(0, xx)
    def _(step):
        base = 2 * (xx - 1 - step)
        kv_twin(base + core).wait_send()


def on_device(
    hidden_in,
    gain_attn,
    gain_mlp,
    w_qkv,
    w_attn_out,
    w_mlp_in,
    w_mlp_out,
    segment_ids,
    positions,
    kv_prefill,
    page_source,
):
    rot_dims = HD // 4
    powers = np.arange(rot_dims // 2, dtype=np.float32) * np.float32(2.0) / np.float32(rot_dims)
    freqs = np.power(np.float32(10000.0), -powers).astype(np.float32)
    freqs = jnp.asarray(np.concatenate([freqs, np.arange(96, dtype=np.float32)])[None, :])
    vmem = pl.BlockSpec(memory_space=pltpu.VMEM)
    hbm = pl.BlockSpec(memory_space=pl.ANY)
    smem = pl.BlockSpec(memory_space=pltpu.SMEM)
    out, pages = pl.pallas_call(
        layer_kernel,
        name="layer",
        out_shape=(
            jax.ShapeDtypeStruct((4, 256, 2048), BF16),
            jax.ShapeDtypeStruct((8, 1024, 256), BF16),
        ),
        in_specs=[hbm, vmem, vmem, hbm, hbm, hbm, hbm, vmem, vmem, vmem, smem, hbm],
        out_specs=(hbm, hbm),
        scratch_shapes=[
            pltpu.VMEM((1024, 2048), BF16),
            pltpu.VMEM((1024, 2048), BF16),
            pltpu.VMEM((2048, 512), BF16),
            pltpu.VMEM((2048, 512), BF16),
            pltpu.VMEM((512, 2048), BF16),
            pltpu.VMEM((256, 2048), BF16),
            pltpu.VMEM((1024, 512), BF16),
            pltpu.VMEM((1024, 2048), BF16),
            pltpu.VMEM((16, 1024, 128), BF16),
            pltpu.VMEM((16, 1024, 128), BF16),
            pltpu.VMEM((2, 4, 4, 256, 128), BF16),
            pltpu.VMEM((2, 4, 2, 256, 256), BF16),
            pltpu.VMEM((4, 2, 1024, 256), BF16),
            pltpu.VMEM((8, 2, 512, 256), BF16),
            pltpu.VMEM((2, 1024, 128), BF16),
            pltpu.VMEM((1024, 256), BF16),
            pltpu.VMEM((256, 1024), F32),
            pltpu.VMEM((256, 1024), BF16),
            pltpu.VMEM((8, 1024), F32),
            pltpu.VMEM((8, 1024), F32),
            pltpu.VMEM((8, 1024), F32),
            pltpu.VMEM((4, 2, 128, 640), BF16),
            pltpu.VMEM((4, 2, 128, 640), BF16),
            pltpu.VMEM((4, 2, 128, 640), BF16),
            pltpu.VMEM((4, 2, 128, 640), BF16),
            pltpu.VMEM((4, 256, 640), BF16),
            pltpu.VMEM((4, 2, 32, 640), BF16),
            pltpu.VMEM((4, 2, 32, 640), BF16),
            pltpu.VMEM((4, 2, 32, 640), BF16),
            pltpu.VMEM((4, 2, 32, 640), BF16),
            pltpu.VMEM((1024, 128), F32),
            pltpu.VMEM((1024, 128), F32),
            pltpu.VMEM((1, 1024), jnp.int32),
            pltpu.SemaphoreType.DMA((48,)),
            pltpu.SemaphoreType.DMA((180,)),
            pltpu.SemaphoreType.DMA((180,)),
            pltpu.SemaphoreType.DMA((16,)),
            pltpu.SemaphoreType.DMA((8, 3)),
        ],
        compiler_params=pltpu.CompilerParams(
            collective_id=0, has_side_effects=True, vmem_limit_bytes=67043328
        ),
    )(
        hidden_in,
        gain_attn[None, :],
        gain_mlp[None, :],
        w_qkv,
        w_attn_out,
        w_mlp_in,
        w_mlp_out,
        freqs,
        segment_ids[None, :],
        positions[None, :],
        page_source,
        kv_prefill.reshape(16, 1024, 128),
    )
    return (out.reshape(1024, 2048), pages.reshape(8, 8, 2, 64, 256))


def solution(mesh):
    placed = (
        P("seq", None),
        P(),
        P(),
        P(None, None, "tensor"),
        P("tensor", None),
        P(None, "tensor"),
        P("tensor", None),
        P("seq"),
        P("seq"),
        P("seq", None, None, None, "tensor"),
        P(),
    )
    return jax.shard_map(
        on_device,
        mesh=mesh,
        in_specs=placed,
        out_specs=(P("seq", None), P("tensor", None, None, None, "seq")),
        check_vma=False,
    )
```

```python
import jax
import jax.numpy as jnp
import numpy as np
from jax import lax
from jax.experimental import pallas as pl
from jax.experimental.pallas import tpu as pltpu
from jax.sharding import PartitionSpec as P

MESH = pl.DeviceIdType.MESH
F32 = jnp.float32
BF16 = jnp.bfloat16
HD = 256
LOW = -1e30
MASKED = -3e30
TT = (((1,), (1,)), ((), ()))
FF = (((0,), (0,)), ((), ()))


def layer_kernel(
    x_hbm,
    ga_ref,
    gm_ref,
    wqkv_hbm,
    wo_hbm,
    wi_hbm,
    w2_hbm,
    freq_ref,
    seg_ref,
    pos_ref,
    psrc_ref,
    kv_hbm,
    out_v,
    kvout_v,
    x_v,
    na_v,
    wcat_v,
    wi_v,
    w2_v,
    wo_v,
    hid_v,
    part_v,
    kvin_v,
    kvs_v,
    bufa_v,
    bufb_v,
    kvx_v,
    kvbuf_v,
    stage_v,
    q_v,
    acc_v,
    att_v,
    stat_v,
    mine_v,
    theirs_v,
    direct_v,
    relay_v,
    merged_v,
    direct2_v,
    relay2_v,
    merged2_v,
    cos_v,
    sin_v,
    first_v,
    lsem,
    ssem,
    rsem,
    kvs_sem,
    kvr_sem,
):
    seq = lax.axis_index("seq")
    ten = lax.axis_index("tensor")
    xx = seq // 2
    core = lax.rem(seq, 2)
    yy = ten // 4
    zz = lax.rem(ten, 4)
    half = lax.rem(ten, 2)
    zh = zz // 2

    def around(value, step):
        return lax.rem(value + step + 4, 4)

    def dev(x_=None, c_=None, y_=None, z_=None):
        x_ = xx if x_ is None else x_
        c_ = core if c_ is None else c_
        y_ = yy if y_ is None else y_
        z_ = zz if z_ is None else z_
        return (x_ * 2 + c_, y_ * 4 + z_)

    counter = [0]
    pending = []

    def remote(src, dst, device):
        index = counter[0]
        counter[0] += 1
        copy = pltpu.make_async_remote_copy(
            src_ref=src,
            dst_ref=dst,
            send_sem=ssem.at[index],
            recv_sem=rsem.at[index],
            device_id=device,
            device_id_type=MESH,
        )
        pending.append(copy)
        return copy

    local_count = [0]

    def local(src, dst):
        index = local_count[0]
        local_count[0] += 1
        copy = pltpu.make_async_copy(src, dst, lsem.at[index])
        copy.start()
        return copy

    barrier = pltpu.get_barrier_semaphore()
    peers = [dev(y_=around(yy, k)) for k in (1, 2, 3)]
    peers += [dev(z_=around(zz, k)) for k in (1, 2, 3)]
    peers += [(lax.rem(seq + k, 8), ten) for k in range(1, 8)]
    for peer in peers:
        pl.semaphore_signal(barrier, inc=1, device_id=peer, device_id_type=MESH)

    load_kv = local(kv_hbm, kvin_v)
    load_x = local(x_hbm, x_v)
    q_cols = pl.ds(pl.multiple_of(256 + half * 128, 128), 128)
    load_w = [local(wqkv_hbm.at[1], wcat_v.at[:, 0:128]), local(wqkv_hbm.at[2], wcat_v.at[:, 128:256])]
    load_w.append(local(wqkv_hbm.at[0], wcat_v.at[:, q_cols]))
    load_wi = local(wi_hbm, wi_v)
    load_w2 = local(w2_hbm, w2_v)
    own_rows = pl.ds(pl.multiple_of(half * 128, 128), 128)
    load_wo = local(wo_hbm, wo_v.at[own_rows, :])

    load_kv.wait()

    @pl.loop(0, 16)
    def _(group):
        kvs_v[group] = kvin_v[lax.rem(psrc_ref[group * 8 + seq], 16)]

    pl.semaphore_wait(barrier, len(peers))

    partner = dev(z_=zz + 1 - 2 * half)
    twin = (seq + 1 - 2 * core, ten)

    wo_piece = pl.ds(pl.multiple_of(seq * 16, 16), 16)
    wq_piece = pl.ds(pl.multiple_of(seq * 256, 256), 256)
    pair_weights = [
        remote(wo_hbm.at[wo_piece], wo_v.at[pl.ds(pl.multiple_of(half * 128 + seq * 16, 16), 16)], partner),
        remote(wqkv_hbm.at[0, wq_piece], wcat_v.at[wq_piece, q_cols], partner),
    ]
    for copy in pair_weights:
        copy.start()
    wo_here = wo_v.at[pl.ds(pl.multiple_of((1 - half) * 128 + seq * 16, 16), 16)]
    wq_here = wcat_v.at[wq_piece, pl.ds(pl.multiple_of(256 + (1 - half) * 128, 128), 128)]
    seq_weights = [
        remote(piece, piece, (lax.rem(seq + k, 8), ten)) for piece in (wq_here, wo_here) for k in (1, 2, 7, 6, 3, 5, 4)
    ]

    col_half = pl.ds(pl.multiple_of(half * 128, 128), 128)

    def low(part):
        return pl.ds(part * 256, 256)

    def high(part):
        return pl.ds(512 + part * 256, 256)

    def y_first(part):
        copies = [
            remote(kvs_v.at[pl.ds(around(yy, k) * 4, 4), low(part)], bufa_v.at[part, yy], dev(y_=around(yy, k)))
            for k in (1, 3, 2)
        ]
        for copy in copies:
            copy.start()
        return copies, [local(kvs_v.at[pl.ds(yy * 4, 4), low(part)], bufa_v.at[part, yy])]

    def then_z(part):
        return [
            remote(bufa_v.at[part, :, around(zz, k)], kvx_v.at[:, zh, low(part), col_half], dev(z_=around(zz, k)))
            for k in (1, 3, 2)
        ]

    def then_z_own(part):
        return [local(bufa_v.at[part, :, zz], kvx_v.at[:, zh, low(part), col_half])]

    away = 2 * half - 1

    def z_first(part):
        return [
            [
                remote(
                    kvs_v.at[y4 * 4 + around(zz, k), high(part)],
                    bufb_v.at[part, y4, zh, :, col_half],
                    dev(z_=around(zz, k)),
                )
                for y4 in range(4)
            ]
            for k in (away, -away, 2)
        ]

    def z_own(part):
        return [local(kvs_v.at[y4 * 4 + zz, high(part)], bufb_v.at[part, y4, zh, :, col_half]) for y4 in range(4)]

    def then_y(part):
        copies = [
            remote(bufb_v.at[part, around(yy, k)], kvx_v.at[yy, :, high(part), :], dev(y_=around(yy, k)))
            for k in (1, 3, 2)
        ]
        for copy in copies:
            copy.start()
        return copies, [local(bufb_v.at[part, yy], kvx_v.at[yy, :, high(part), :])]

    def along_x(rows):
        copies = []
        for k in (1, 2, 7, 6, 3, 5, 4):
            to = lax.rem(seq + k, 8)
            copies.append(
                remote(kvx_v.at[to // 2, lax.rem(to, 2), rows], kvout_v.at[seq, rows], (to, ten))
            )
            copies[-1].start()
        return copies, [local(kvx_v.at[xx, core, rows], kvout_v.at[seq, rows])]

    def arrived(stage):
        copies, own = stage
        for copy in own:
            copy.wait()
        for copy in copies:
            copy.wait_recv()

    y_one = [y_first(0), y_first(1)]
    z_sends = [z_first(0), z_first(1)]
    for part in (0, 1):
        for copy in z_sends[part][0]:
            copy.start()

    positions = pos_ref[...]
    freqs = jnp.broadcast_to(freq_ref[...], (128, 128)).T[0:32, 0:1]
    angles = freqs * positions.astype(F32)
    cosine = jnp.cos(angles)
    sine = jnp.sin(angles)
    cos_v[...] = jnp.concatenate([cosine, cosine, jnp.ones((64, 1024), F32)], axis=0).T
    sin_v[...] = jnp.concatenate([-sine, sine, jnp.zeros((64, 1024), F32)], axis=0).T
    tokens = seq * 1024 + lax.broadcasted_iota(jnp.int32, (1, 1024), 1)
    first_v[...] = jnp.where(seg_ref[...] == 0, 0, tokens - positions)

    load_x.wait()
    for copy in load_w:
        copy.wait()
    ga = ga_ref[...]
    gm = gm_ref[...]

    def normed_rows(rows):
        values = x_v[rows, :].astype(F32)
        mean = jnp.mean(values, axis=-1, keepdims=True)
        centered = values - mean
        spread = jnp.mean(centered * centered, axis=-1, keepdims=True)
        return centered * lax.rsqrt(spread + 1e-05)

    def turned(values_in, rows):
        lanes = lax.broadcasted_iota(jnp.int32, (256, 128), 1)
        other = jnp.where(lanes < 32, pltpu.roll(values_in, 96, 1), pltpu.roll(values_in, 32, 1))
        return values_in * cos_v[rows, :] + other * sin_v[rows, :]

    def keys_values(first_step, last_step):
        @pl.loop(first_step, last_step)
        def _(step):
            start = lax.rem(step * 256 + (1 - half) * 512, 1024)
            rows = pl.ds(pl.multiple_of(start, 256), 256)
            normed = normed_rows(rows)
            na = (normed * ga).astype(BF16)
            na_v[rows, :] = na
            nm = (normed * gm).astype(BF16)
            for c in range(16):
                kvin_v[c, rows, :] = nm[:, c * 128 : (c + 1) * 128]
            kv = jnp.dot(na, wcat_v[:, 0:256], preferred_element_type=F32)
            keys = kv[:, 0:128]
            keys = jnp.where(jnp.broadcast_to(half, (256, 128)) == 0, turned(keys, rows), keys)
            stage_v[0, rows, :] = keys.astype(BF16)
            stage_v[1, rows, :] = kv[:, 128:256].astype(BF16)

    own_keys = pl.ds(pl.multiple_of(half * 512, 512), 512)
    kv_cross = []
    for step in (0, 1):
        keys_values(step, step + 1)
        cross_keys = pl.ds(pl.multiple_of((1 - half) * 512 + step * 256, 256), 256)
        kv_cross.append(
            remote(stage_v.at[:, cross_keys], kvbuf_v.at[seq, :, pl.ds(step * 256, 256), col_half], partner)
        )
        kv_cross[-1].start()
    for copy in pair_weights:
        copy.wait_recv()
    for copy in seq_weights:
        copy.start()
    z_one = []
    for part in (0, 1):
        for copies in z_sends[part][1:]:
            for copy in copies:
                copy.start()
        z_one.append(([copy for copies in z_sends[part] for copy in copies], z_own(part)))
    keys_values(2, 4)
    kv_own = local(stage_v.at[:, own_keys], kvbuf_v.at[seq, :, :, col_half])

    load_wi.wait()

    def mlp_in(first_step):
        @pl.loop(first_step, first_step + 4)
        def _(step):
            rows = pl.ds(pl.multiple_of(step * 256, 256), 256)
            nm = jnp.concatenate([kvin_v[c, rows, :] for c in range(16)], axis=1)
            hidden = jnp.dot(nm, wi_v[...], preferred_element_type=F32)
            hid_v[rows, :] = (0.5 * hidden * (1.0 + lax.erf(hidden * (0.5**0.5)))).astype(BF16)

    kv_own.wait()
    for copy in kv_cross:
        copy.wait_recv()

    def kv_part(slot, part, device, index):
        return pltpu.make_async_remote_copy(
            src_ref=kvbuf_v.at[slot, part],
            dst_ref=kvbuf_v.at[slot, part],
            send_sem=kvs_sem.at[index],
            recv_sem=kvr_sem.at[slot, part],
            device_id=device,
            device_id_type=MESH,
        )

    def kv_twin(slot):
        return pltpu.make_async_remote_copy(
            src_ref=kvbuf_v.at[slot],
            dst_ref=kvbuf_v.at[slot],
            send_sem=kvs_sem.at[8 + slot],
            recv_sem=kvr_sem.at[slot, 2],
            device_id=twin,
            device_id_type=MESH,
        )

    def sends(copies):
        def start():
            for copy in copies:
                copy.start()

        def wait():
            for copy in copies:
                copy.wait_send()

        return start, wait

    chips = [dev(x_=k) for k in range(4)]
    own_out = [
        sends([kv_part(seq, 1, chips[3], 0), kv_part(seq, 0, chips[1], 1), kv_part(seq, 1, chips[1], 2), kv_part(seq, 0, chips[3], 3)]),
        sends([kv_part(seq, 1, chips[0], 0), kv_part(seq, 0, chips[2], 1), kv_part(seq, 1, chips[2], 2)]),
        sends([kv_part(seq, 0, chips[3], 0), kv_part(seq, 1, chips[3], 1)]),
    ]
    passed_on = [
        kv_part(2 + core, 1, chips[3], 4),
        kv_part(core, 0, chips[2], 4),
        kv_part(2 + core, 0, chips[3], 4),
        kv_part(core, 1, chips[2], 4),
    ]
    for k in range(3):
        pl.when(xx == k)(own_out[k][0])
    pl.when(core == 0)(kv_twin(seq).start)

    mlp_in(0)

    for copy in seq_weights[:7]:
        copy.wait_recv()

    @pl.loop(0, 4)
    def _(step):
        rows = pl.ds(pl.multiple_of(step * 256, 256), 256)
        q = jnp.dot(na_v[rows, :], wcat_v[:, 256:512], preferred_element_type=F32) * (HD**-0.5)
        q_v[rows, 0:128] = turned(q[:, 0:128], rows).astype(BF16)
        q_v[rows, 128:256] = q[:, 128:256].astype(BF16)

    load_w2.wait()

    @pl.loop(0, 4)
    def _(step):
        rows = pl.ds(pl.multiple_of(step * 256, 256), 256)
        part_v[rows, :] = jnp.dot(hid_v[rows, :], w2_v[...], preferred_element_type=F32).astype(BF16)

    z_two = []
    for part in (0, 1):
        arrived(y_one[part])
        z_two.append((then_z(part), then_z_own(part)))
    for copy in z_two[0][0]:
        copy.start()

    acc_v[...] = jnp.zeros_like(acc_v)
    stat_v[0:1, :] = jnp.full((1, 1024), LOW, F32)
    stat_v[1:2, :] = jnp.zeros((1, 1024), F32)

    def attend(slot, first_step=0):
        keys = kvbuf_v[slot, 0]
        vals = kvbuf_v[slot, 1]
        vals_t = vals.T
        key_ids = slot * 1024 + half * 512 + lax.broadcasted_iota(jnp.int32, (512, 1), 0)

        @pl.loop(first_step, 4)
        def _(step):
            cols = pl.ds(pl.multiple_of(step * 256, 256), 256)
            scores = lax.dot_general(keys, q_v[cols, :], TT, preferred_element_type=F32)
            query_ids = seq * 1024 + step * 256 + lax.broadcasted_iota(jnp.int32, (1, 256), 1)
            allowed = (key_ids >= first_v[:, cols]) & (key_ids <= query_ids)
            scores = jnp.where(allowed, scores, MASKED)
            old_max = stat_v[0:1, cols]
            new_max = jnp.maximum(old_max, jnp.max(scores, axis=0, keepdims=True))
            weights = jnp.exp(scores - new_max)
            keep = jnp.exp(old_max - new_max)
            stat_v[0:1, cols] = new_max
            stat_v[1:2, cols] = stat_v[1:2, cols] * keep + jnp.sum(weights, axis=0, keepdims=True)
            acc_v[:, cols] = acc_v[:, cols] * keep + jnp.dot(
                vals_t, weights.astype(BF16), preferred_element_type=F32
            )

    attend(seq, 2 * half)

    for k in range(4):

        @pl.when(xx == k)
        def _(k=k):
            passed_on[k].wait_recv()
            passed_on[k].start()

    arrived(z_one[0])
    y_two = [then_y(0)]

    @pl.when(core == 1)
    def _():
        kv_twin(seq - 1).wait_recv()
        attend(seq - 1)

    arrived(z_one[1])
    y_two.append(then_y(1))

    @pl.loop(0, xx)
    def _(step):
        base = 2 * (xx - 1 - step)
        pl.when(jnp.logical_or(step > 0, xx == 3))(kv_part(base + core, 0, twin, 0).wait_recv)
        pl.when(jnp.logical_or(base > 0, xx < 3))(kv_part(base + core, 1, twin, 0).wait_recv)
        kv_twin(base + core).start()
        attend(base + core)
        kv_twin(base + 1 - core).wait_recv()
        attend(base + 1 - core)

    mine_v[...] = stat_v[...]
    stat_cross = remote(mine_v, theirs_v, partner)
    stat_cross.start()
    load_wo.wait()
    for copy in seq_weights[7:]:
        copy.wait_recv()
    stat_cross.wait_recv()
    top = jnp.maximum(stat_v[0:1, :], theirs_v[0:1, :])
    mine = jnp.exp(stat_v[0:1, :] - top)
    total = stat_v[1:2, :] * mine + theirs_v[1:2, :] * jnp.exp(theirs_v[0:1, :] - top)
    stat_v[0:1, :] = mine / total

    att_v[...] = (acc_v[...] * stat_v[0:1, :]).astype(BF16)

    def project(group):
        cols = cols_of(group)

        @pl.loop(0, 4)
        def _(step):
            rows = pl.ds(pl.multiple_of(step * 256, 256), 256)
            summed = lax.dot_general(att_v[:, rows], wo_v[:, cols], FF, preferred_element_type=F32)
            part_v[rows, cols] = (part_v[rows, cols].astype(F32) + summed).astype(BF16)

    widths = (512, 512, 512, 512)
    starts = (0, 512, 1024, 1536)

    def cols_of(which):
        return pl.ds(starts[which], widths[which])

    def axis_dev(which, step, first):
        along_y = (which % 2 == 0) == first
        return dev(y_=around(yy, step)) if along_y else dev(z_=around(zz, step))

    def scatter(which, first, source, size, direct, relay, merged):
        pos = yy if (which % 2 == 0) == first else zz
        hs = size // 2
        wide = pl.ds(0, widths[which])
        direct, relay, merged = ([buf.at[which, k, :, wide] for k in (0, 1)] for buf in (direct, relay, merged))

        def piece(step, part):
            begin = around(pos, step) * size + part * hs
            return source(pl.ds(pl.multiple_of(begin, hs), hs))

        plus = axis_dev(which, 1, first)
        minus = axis_dev(which, -1, first)
        r0 = remote(piece(2, 0), relay[0], plus)
        r1 = remote(piece(2, 1), relay[1], minus)
        d0 = remote(piece(1, 1), direct[0], plus)
        d1 = remote(piece(-1, 0), direct[1], minus)
        m0 = remote(relay[0], merged[0], plus)
        m1 = remote(relay[1], merged[1], minus)

        def one():
            for copy in (r0, r1, d0, d1):
                copy.start()

        def two():
            r0.wait_recv()
            relay[0][...] = (piece(1, 0)[...].astype(F32) + relay[0][...].astype(F32)).astype(BF16)
            m0.start()
            r1.wait_recv()
            relay[1][...] = (piece(-1, 1)[...].astype(F32) + relay[1][...].astype(F32)).astype(BF16)
            m1.start()

        def three():
            d0.wait_recv()
            d1.wait_recv()
            m0.wait_recv()
            m1.wait_recv()
            lower = piece(0, 0)[...].astype(F32) + direct[1][...].astype(F32) + merged[0][...].astype(F32)
            upper = piece(0, 1)[...].astype(F32) + direct[0][...].astype(F32) + merged[1][...].astype(F32)
            return lower, upper

        return one, two, three

    groups = range(4)
    base_of = (yy * 256, zz * 256) * 2

    def own_chunk(w, begin, size):
        return part_v.at[pl.ds(pl.multiple_of(base_of[w] + begin, 32), size), cols_of(w)]

    def fold(w, begin, value):
        part_v[pl.ds(pl.multiple_of(base_of[w] + begin, 128), 128), cols_of(w)] = value.astype(BF16)

    first_stage = [
        scatter(w, True, lambda rows, w=w: part_v.at[rows, cols_of(w)], 256, direct_v, relay_v, merged_v)
        for w in groups
    ]
    second_stage = [
        scatter(w, False, lambda rows, w=w: own_chunk(w, rows.start, rows.size), 64, direct2_v, relay2_v, merged2_v)
        for w in groups
    ]
    for w in groups:
        project(w)
        first_stage[w][0]()
    arrived(y_two[0])
    x_three = [along_x(high(0))]
    for w in groups:
        first_stage[w][1]()
    for copy in z_two[1][0][:2]:
        copy.start()
    arrived(z_two[0])
    x_three.append(along_x(low(0)))
    for w in groups:
        lower, upper = first_stage[w][2]()
        fold(w, 0, lower)
        fold(w, 128, upper)
        second_stage[w][0]()
    z_two[1][0][2].start()
    arrived(y_two[1])
    x_three.append(along_x(high(1)))
    for w in groups:
        second_stage[w][1]()

    small_of = (zz, yy) * 2

    def gather(which, first, base, size):
        pos = yy if (which % 2 == 0) == first else zz
        hs = size // 2

        def rows_at(step, part=None):
            begin = base + around(pos, step) * size
            if part is None:
                return out_v.at[pl.ds(pl.multiple_of(begin, size), size), cols_of(which)]
            return out_v.at[pl.ds(pl.multiple_of(begin + part * hs, hs), hs), cols_of(which)]

        plus = axis_dev(which, 1, first)
        minus = axis_dev(which, -1, first)
        own = rows_at(0)
        g0 = remote(own, own, plus)
        g1 = remote(own, own, minus)
        f0 = remote(rows_at(-1, 0), rows_at(-1, 0), plus)
        f1 = remote(rows_at(1, 1), rows_at(1, 1), minus)

        def one():
            g0.start()
            g1.start()

        def two():
            g0.wait_recv()
            f0.start()
            g1.wait_recv()
            f1.start()

        def three():
            f0.wait_recv()
            f1.wait_recv()

        return one, two, three

    small_gather = [gather(w, False, base_of[w], 64) for w in groups]
    large_gather = [gather(w, True, 0, 256) for w in groups]
    for w in groups:
        lower, upper = second_stage[w][2]()
        begin = base_of[w] + small_of[w] * 64
        for part, value in ((0, lower), (1, upper)):
            rows = pl.ds(pl.multiple_of(begin + part * 32, 32), 32)
            out_v[rows, cols_of(w)] = (x_v[rows, cols_of(w)].astype(F32) + value).astype(BF16)
        small_gather[w][0]()
    arrived(z_two[1])
    x_three.append(along_x(low(1)))
    for w in groups:
        small_gather[w][1]()
    for w in groups:
        small_gather[w][2]()
        large_gather[w][0]()
    for w in groups:
        large_gather[w][1]()
    for w in groups:
        large_gather[w][2]()
    for stage in x_three:
        arrived(stage)
    for copy in pending:
        copy.wait_send()
    for k in range(3):
        pl.when(xx == k)(own_out[k][1])
    for k in range(4):
        pl.when(xx == k)(passed_on[k].wait_send)
    pl.when(core == 0)(kv_twin(seq).wait_send)

    @pl.loop(0, xx)
    def _(step):
        base = 2 * (xx - 1 - step)
        kv_twin(base + core).wait_send()


def on_device(
    hidden_in,
    gain_attn,
    gain_mlp,
    w_qkv,
    w_attn_out,
    w_mlp_in,
    w_mlp_out,
    segment_ids,
    positions,
    kv_prefill,
    page_source,
):
    rot_dims = HD // 4
    powers = np.arange(rot_dims // 2, dtype=np.float32) * np.float32(2.0) / np.float32(rot_dims)
    freqs = np.power(np.float32(10000.0), -powers).astype(np.float32)
    freqs = jnp.asarray(np.concatenate([freqs, np.arange(96, dtype=np.float32)])[None, :])
    vmem = pl.BlockSpec(memory_space=pltpu.VMEM)
    hbm = pl.BlockSpec(memory_space=pl.ANY)
    smem = pl.BlockSpec(memory_space=pltpu.SMEM)
    out, pages = pl.pallas_call(
        layer_kernel,
        name="layer",
        out_shape=(
            pltpu.VMEM((1024, 2048), BF16),
            pltpu.VMEM((8, 1024, 256), BF16),
        ),
        in_specs=[hbm, vmem, vmem, hbm, hbm, hbm, hbm, vmem, vmem, vmem, smem, hbm],
        out_specs=(vmem, vmem),
        scratch_shapes=[
            pltpu.VMEM((1024, 2048), BF16),
            pltpu.VMEM((1024, 2048), BF16),
            pltpu.VMEM((2048, 512), BF16),
            pltpu.VMEM((2048, 512), BF16),
            pltpu.VMEM((512, 2048), BF16),
            pltpu.VMEM((256, 2048), BF16),
            pltpu.VMEM((1024, 512), BF16),
            pltpu.VMEM((1024, 2048), BF16),
            pltpu.VMEM((16, 1024, 128), BF16),
            pltpu.VMEM((16, 1024, 128), BF16),
            pltpu.VMEM((2, 4, 4, 256, 128), BF16),
            pltpu.VMEM((2, 4, 2, 256, 256), BF16),
            pltpu.VMEM((4, 2, 1024, 256), BF16),
            pltpu.VMEM((8, 2, 512, 256), BF16),
            pltpu.VMEM((2, 1024, 128), BF16),
            pltpu.VMEM((1024, 256), BF16),
            pltpu.VMEM((256, 1024), F32),
            pltpu.VMEM((256, 1024), BF16),
            pltpu.VMEM((8, 1024), F32),
            pltpu.VMEM((8, 1024), F32),
            pltpu.VMEM((8, 1024), F32),
            pltpu.VMEM((4, 2, 128, 512), BF16),
            pltpu.VMEM((4, 2, 128, 512), BF16),
            pltpu.VMEM((4, 2, 128, 512), BF16),
            pltpu.VMEM((4, 2, 32, 512), BF16),
            pltpu.VMEM((4, 2, 32, 512), BF16),
            pltpu.VMEM((4, 2, 32, 512), BF16),
            pltpu.VMEM((1024, 128), F32),
            pltpu.VMEM((1024, 128), F32),
            pltpu.VMEM((1, 1024), jnp.int32),
            pltpu.SemaphoreType.DMA((48,)),
            pltpu.SemaphoreType.DMA((180,)),
            pltpu.SemaphoreType.DMA((180,)),
            pltpu.SemaphoreType.DMA((16,)),
            pltpu.SemaphoreType.DMA((8, 3)),
        ],
        compiler_params=pltpu.CompilerParams(
            collective_id=0, has_side_effects=True, vmem_limit_bytes=58600000
        ),
    )(
        hidden_in,
        gain_attn[None, :],
        gain_mlp[None, :],
        w_qkv,
        w_attn_out,
        w_mlp_in,
        w_mlp_out,
        freqs,
        segment_ids[None, :],
        positions[None, :],
        page_source,
        kv_prefill.reshape(16, 1024, 128),
    )
    return (out, pages.reshape(8, 8, 2, 64, 256))


def solution(mesh):
    placed = (
        P("seq", None),
        P(),
        P(),
        P(None, None, "tensor"),
        P("tensor", None),
        P(None, "tensor"),
        P("tensor", None),
        P("seq"),
        P("seq"),
        P("seq", None, None, None, "tensor"),
        P(),
    )
    return jax.shard_map(
        on_device,
        mesh=mesh,
        in_specs=placed,
        out_specs=(P("seq", None), P("tensor", None, None, None, "seq")),
        check_vma=False,
    )
```
